32 devices in a mesh: grp: 2 (over y), wa: 4 (over z), col: 2 (over x), row: 2 (over core).
Axes of the slice: x: 2, y: 2, z: 4, core: 2. Of those that a mesh axis runs over, the one named last changes fastest.
Arguments:
- walkers: bfloat16 [64, 1024, 384], P(('grp', 'wa', 'col', 'row')), parts along dimension 0, may hold values from -2 to 2
- intersection_inverse: bfloat16 [64, 384, 384], P(('grp', 'wa', 'col', 'row')), parts along dimension 0, may hold values from -0.3125 to 0.3125
- noise_index: int32 [64, 64], P(('grp', 'wa', 'col', 'row')), parts along dimension 0, may hold values from 0 to 65535
- cholesky: bfloat16 [64, 1024, 1024], P(None, ('wa', 'col')), may hold values from -0.21875 to 0.21875
Outputs:
- walkers_new: bfloat16 [64, 1024, 384], P(('grp', 'wa', 'col', 'row')), parts along dimension 0
- log_weight: float32 [64], P(('grp', 'wa', 'col', 'row')), parts along dimension 0
The draws below stay inside these ranges and needn't reach their ends.
There are 2 independent parts, one for each index of `grp`. The reference program is written for one: setup_inputs(seed, part) draws one part's arguments, and reference() takes and returns one part's arrays. A program takes and returns all parts, laid end to end along the dimension named above; an argument that names none is the same for every part. Nothing has to cross between parts.
All inputs are finite; a program needn't handle non-finite values.
Results may differ from the reference program's by a relative error of at most 0.006.
Values may be sent and summed in bfloat16 or wider, within the bound.
A program may use at most 128 MiB of HBM per device.

```python
import jax
import jax.numpy as jnp
from jax import lax

N = 1024
NE = 384
NCHOL = 64
NOISE_LEVELS = 65536
W = 32


def place_ends(array, rng, least, top_value):
    index_at = [jax.random.randint(jax.random.fold_in(rng, axis), (), 0, length) for axis, length in enumerate(array.shape)]
    widest = array.shape.index(max(array.shape))
    neighbour = index_at[:widest] + [(index_at[widest] + 1) % array.shape[widest]] + index_at[widest + 1:]
    return array.at[tuple(index_at)].set(least).at[tuple(neighbour)].set(top_value)


def block_levels(rng, dims, shards, least, largest):
    def one(position, shards_of):
        steps = jax.random.uniform(jax.random.fold_in(jax.random.fold_in(rng, 6), position), (shards_of,), jnp.float32, least / len(shards), largest / len(shards))
        return jnp.repeat(jnp.exp(steps), dims[position] // shards_of).reshape((-1,) + (1,) * (len(dims) - position - 1))

    level = one(*shards[0])
    for cut in shards[1:]:
        level = level * one(*cut)
    return level


def centred(own_key, shape, spread, limit, split=(), kind=jnp.bfloat16):
    values = spread * jax.random.normal(own_key, shape, jnp.float32)
    if split:
        values = values * block_levels(own_key, shape, split, -0.22, 0.18)
    return jnp.clip(values, -limit, limit).astype(kind)


def setup_inputs(seed: int = 0, part: int = 0) -> dict:
    key_list = jax.random.split(jax.random.key(seed), 5)
    part_keys = jax.random.split(jax.random.fold_in(key_list[4], part), 5)
    return {
        "walkers": centred(part_keys[0], (W, N, NE), 0.35, 2.0, ((0, 16),)),
        "intersection_inverse": centred(part_keys[1], (W, NE, NE), NE ** -0.5, 0.3125, ((0, 16),)),
        "noise_index": place_ends(jax.random.randint(part_keys[2], (W, NCHOL), 0, NOISE_LEVELS), jax.random.fold_in(part_keys[2], 1), 0, NOISE_LEVELS - 1).astype(jnp.int32),
        "cholesky": centred(key_list[3], (NCHOL, N, N), (12 * NCHOL) ** -0.5, 0.21875, ((1, 8),)),
    }


STEP_ROOT = 0.1
BIAS_CAP = 1.0
ROOT_TWO = 1.4142135623730951


def normal_quantile(code_row):
    level = (code_row.astype(jnp.float32) + 0.5) / NOISE_LEVELS
    return ROOT_TWO * lax.erf_inv(2.0 * level - 1.0)


def reference(walkers, intersection_inverse, noise_index, cholesky):
    half_rows = cholesky[:, :, :NE].reshape(NCHOL, N * NE)
    full_rows = cholesky.reshape(NCHOL, N * N)

    def advance(packed):
        walker_mat, inverse_mat, code_row = packed
        green_half = jnp.dot(walker_mat, inverse_mat, preferred_element_type=jnp.float32).astype(jnp.bfloat16)
        bias_sum = jnp.dot(half_rows, green_half.reshape(N * NE), preferred_element_type=jnp.float32)
        force_bias = jnp.clip(STEP_ROOT * bias_sum, -BIAS_CAP, BIAS_CAP)
        noise = normal_quantile(code_row)
        shifted = noise - force_bias
        log_step = jnp.sum(shifted * force_bias - 0.5 * force_bias * force_bias)
        field = shifted.astype(jnp.bfloat16)
        potential = jnp.dot(field, full_rows, preferred_element_type=jnp.float32).astype(jnp.bfloat16).reshape(N, N)
        running = walker_mat.astype(jnp.float32)
        factor_term = walker_mat
        for degree in range(1, 5):
            product = (-STEP_ROOT / degree) * jnp.dot(potential, factor_term, preferred_element_type=jnp.float32)
            running = running + product
            factor_term = product.astype(jnp.bfloat16)
        return running.astype(jnp.bfloat16), log_step

    walkers_new, log_weight = lax.map(advance, (walkers, intersection_inverse, noise_index))
    return walkers_new, log_weight
```

```python
import functools

import jax
import jax.numpy as jnp
from jax import lax
from jax.experimental import pallas as pl
from jax.experimental.pallas import tpu as pltpu
from jax.sharding import PartitionSpec as P

NOISE_LEVELS = 65536


STEP_ROOT = 0.1
BIAS_CAP = 1.0
ROOT_TWO = 1.4142135623730951


def force_terms(green_tiles, half_tile):
    return jnp.einsum("ksf,gf->ksg", green_tiles, half_tile, preferred_element_type=jnp.float32)


def shift_field(bias_sum, code_block):
    force_bias = jnp.clip(STEP_ROOT * bias_sum, -BIAS_CAP, BIAS_CAP)
    level = (code_block.astype(jnp.float32) + 0.5) / NOISE_LEVELS
    noise = ROOT_TWO * lax.erf_inv(2.0 * level - 1.0)
    shifted = noise - force_bias
    log_step = jnp.sum(shifted * force_bias - 0.5 * force_bias * force_bias, axis=-1)
    return (shifted.astype(jnp.bfloat16), log_step)


def exchange_form(walkers, intersection_inverse, noise_index, cholesky):
    walker_count = walkers.shape[0]
    orbitals = walkers.shape[1]
    electrons = walkers.shape[2]
    vectors = cholesky.shape[0]
    tile_rows = cholesky.shape[1]
    along_wa = lax.axis_size("wa")
    along_col = lax.axis_size("col")
    planes = along_wa * along_col
    green_half = jnp.einsum(
        "kpe,kef->kpf", walkers, intersection_inverse, preferred_element_type=jnp.float32
    ).astype(jnp.bfloat16)
    packed = green_half.reshape(walker_count, planes, tile_rows * electrons)
    half_tile = cholesky[:, :, :electrons].reshape(vectors, tile_rows * electrons)
    partial_sums = force_terms(
        lax.all_to_all(packed, ("wa", "col"), split_axis=1, concat_axis=1, tiled=True), half_tile
    )
    bias_sum = lax.psum(partial_sums, ("wa", "col"))
    gathered = lax.all_gather(noise_index, ("wa", "col"), axis=0, tiled=True)
    gathered = jnp.transpose(gathered.reshape(planes, walker_count, vectors), (1, 0, 2))
    field, log_all = shift_field(bias_sum, gathered)
    log_weight = lax.dynamic_slice_in_dim(log_all, lax.axis_index(("wa", "col")), 1, 1)[:, 0]
    full_tile = cholesky.reshape(vectors, tile_rows * orbitals)
    tiles_out = jnp.einsum(
        "ksg,gf->ksf", field, full_tile, preferred_element_type=jnp.float32
    ).astype(jnp.bfloat16)
    returned = lax.all_to_all(tiles_out, ("wa", "col"), split_axis=1, concat_axis=1, tiled=True)
    potential = returned.reshape(walker_count, orbitals, orbitals)
    running = walkers.astype(jnp.float32)
    factor_term = walkers
    for degree in range(1, 5):
        product = (
            -STEP_ROOT
            / degree
            * jnp.einsum("kpq,kqe->kpe", potential, factor_term, preferred_element_type=jnp.float32)
        )
        running = running + product
        factor_term = product.astype(jnp.bfloat16)
    return (running.astype(jnp.bfloat16), log_weight)


BLOCK = 16
LANES = 128
SUBLANES = 8
MESH = pl.DeviceIdType.MESH


def step_kernel(
    along_wa, along_col, chunks,
    walkers_hbm, inverse_hbm, noise_hbm, chol_hbm, out_ref, log_ref,
    walkers_ref, inverse_ref, noise_ref,
    chol, green_send, green_recv, part_send, part_recv, v_send, v_recv, total, spread, term, running,
    in_sem, chol_sem, gs, gr, ps, pr, vs, vr,
):
    planes = along_wa * along_col
    count, orbitals, electrons = walkers_ref.shape
    blocks, vectors = chol.shape[0], chol.shape[1]
    rows = blocks * BLOCK
    wide = planes * BLOCK
    deep = vectors * BLOCK
    me = lax.axis_index("wa") * along_col + lax.axis_index("col")
    half = planes // 2
    hops = range(1, planes)
    near, far = range(1, half), range(half, planes)

    def peer(d):
        b = me
        for bit in (1 << i for i in range(planes.bit_length() - 1)):
            if d & bit:
                b = b + bit * (1 - 2 * lax.rem(me // bit, 2))
        return b, {"wa": b // along_col, "col": lax.rem(b, along_col)}

    loads = [
        pltpu.make_async_copy(chol_hbm.at[:, pl.ds(b * BLOCK, BLOCK), :], chol.at[b], chol_sem.at[b])
        for b in range(blocks)
    ]
    barrier = pltpu.get_barrier_semaphore()
    for d in hops:
        pl.semaphore_signal(barrier, inc=1, device_id=peer(d)[1], device_id_type=MESH)
    inputs = [
        pltpu.make_async_copy(hbm.at[k], ref.at[k], in_sem.at[i, k])
        for k in range(count)
        for i, (hbm, ref) in enumerate(((walkers_hbm, walkers_ref), (inverse_hbm, inverse_ref)))
    ]
    inputs.append(pltpu.make_async_copy(noise_hbm, noise_ref, in_sem.at[2, 0]))
    for load in inputs:
        load.start()

    strip = half * rows

    side = me // half

    def green_of(k, base):
        at = pl.ds(pl.multiple_of(base, strip), strip)
        green_send[k, at, :] = jnp.dot(
            walkers_ref[k, at, :], inverse_ref[k], preferred_element_type=jnp.float32
        ).astype(jnp.bfloat16)

    def send_green(k, those):
        copies = []
        for d in those:
            b, device = peer(d)
            copy = pltpu.make_async_remote_copy(
                src_ref=green_send.at[k, pl.ds(pl.multiple_of(b * rows, rows), rows), :],
                dst_ref=green_recv.at[k, me],
                send_sem=gs.at[k, d],
                recv_sem=gr.at[k, d],
                device_id=device,
                device_id_type=MESH,
            )
            copy.start()
            copies.append(copy)
        return copies

    def keep_green(k):
        green_recv[k, me] = green_send[k, pl.ds(pl.multiple_of(me * rows, rows), rows), :]

    held = half + half // 2
    green_copies = []
    for k in range(count):
        for load in inputs[2 * k : 2 * k + 2]:
            load.wait()
        green_of(k, (1 - side) * strip)
        if k == 0:
            pl.semaphore_wait(barrier, planes - 1)
        green_copies.append(send_green(k, range(half, planes if k == 0 else held) if k < 2 else ()))
        if k == 0:
            for load in loads:
                load.start()
        green_of(k, side * strip)
        green_copies[k] += send_green(k, near if k < 2 else ())
        keep_green(k)
    for load in (inputs[-1], *loads):
        load.wait()

    row_in = lax.broadcasted_iota(jnp.int32, (deep, wide), 0) % BLOCK
    col_in = lax.broadcasted_iota(jnp.int32, (deep, wide), 1) % BLOCK
    pick = (
        lax.broadcasted_iota(jnp.int32, (planes, wide), 1) // BLOCK
        == lax.broadcasted_iota(jnp.int32, (planes, wide), 0)
    ).astype(jnp.float32)

    def noise_of(k):
        level = (noise_ref[k : k + 1, :].astype(jnp.float32) + 0.5) / NOISE_LEVELS
        return ROOT_TWO * lax.erf_inv(2.0 * level - 1.0)

    def partial_of(k):
        total[...] = jnp.zeros_like(total)

        def body(i, carry):
            left = chol[i, :, :, :electrons].reshape(deep, electrons)
            right = green_recv[k, :, pl.ds(pl.multiple_of(i * BLOCK, BLOCK), BLOCK), :].reshape(wide, electrons)
            total[...] += lax.dot_general(
                left, right, (((1,), (1,)), ((), ())), preferred_element_type=jnp.float32
            )
            return carry

        lax.fori_loop(0, blocks, body, 0)
        kept = jnp.where(row_in == col_in, total[...], 0.0).reshape(vectors, BLOCK, wide).sum(axis=1)
        part_send[k, 0, :, :vectors] = lax.dot_general(
            pick, kept, (((1,), (1,)), ((), ())),
            preferred_element_type=jnp.float32, precision=lax.Precision.HIGHEST,
        )
        part_send[k, 1, :, :vectors] = jnp.broadcast_to(noise_of(k), (planes, vectors))

    def send_part(k):
        copies = []
        for d in hops:
            copy = pltpu.make_async_remote_copy(
                src_ref=part_send.at[k],
                dst_ref=part_recv.at[k, me],
                send_sem=ps.at[k, d],
                recv_sem=pr.at[k, d],
                device_id=peer(d)[1],
                device_id_type=MESH,
            )
            copy.start()
            copies.append(copy)
        part_recv[k, me] = part_send[k]
        return copies

    plane_row = lax.broadcasted_iota(jnp.int32, (planes, LANES), 0)

    def spread_field(k):
        bias_sum = part_recv[k, 0, 0]
        noise = jnp.where(plane_row == 0, part_recv[k, 0, 1], 0.0)
        for a in range(1, planes):
            bias_sum = bias_sum + part_recv[k, a, 0]
            noise = jnp.where(plane_row == a, part_recv[k, a, 1], noise)
        force = jnp.clip(STEP_ROOT * bias_sum, -BIAS_CAP, BIAS_CAP)
        shifted = noise - force
        steps = jnp.where(plane_row == me, shifted * force - 0.5 * force * force, 0.0)
        log_ref[k] = jnp.sum(steps)
        field = shifted.astype(jnp.bfloat16)
        tall = (
            lax.broadcasted_iota(jnp.int32, (wide, planes), 0) // BLOCK
            == lax.broadcasted_iota(jnp.int32, (wide, planes), 1)
        ).astype(jnp.float32)
        by_row = jnp.dot(tall, field.astype(jnp.float32), preferred_element_type=jnp.float32)
        out = (
            lax.broadcasted_iota(jnp.int32, (LANES, deep), 1) // BLOCK
            == lax.broadcasted_iota(jnp.int32, (LANES, deep), 0)
        ).astype(jnp.float32).astype(jnp.bfloat16)
        both = jnp.dot(by_row.astype(jnp.bfloat16), out, preferred_element_type=jnp.float32)
        same = (
            lax.broadcasted_iota(jnp.int32, (wide, deep), 0) % BLOCK
            == lax.broadcasted_iota(jnp.int32, (wide, deep), 1) % BLOCK
        )
        spread[...] = jnp.where(same, both, 0.0).astype(jnp.bfloat16)

    each = blocks // chunks
    part_rows = each * BLOCK

    def potential_rows(k, c):
        def body(i, carry):
            b = c * each + i
            tile = jnp.dot(
                spread[...], chol[b].reshape(deep, orbitals), preferred_element_type=jnp.float32
            ).astype(jnp.bfloat16)
            v_send[k, :, pl.ds(pl.multiple_of(b * BLOCK, BLOCK), BLOCK), :] = tile.reshape(
                planes, BLOCK, orbitals
            )
            return carry

        lax.fori_loop(0, each, body, 0)

    def mine(c):
        return pl.ds(pl.multiple_of(me * rows + c * part_rows, BLOCK), part_rows)

    near_copies = [[] for k in range(count)]
    far_copies = [[] for k in range(count)]

    def send_rows(k, c, those, kept):
        for d in those:
            b, device = peer(d)
            copy = pltpu.make_async_remote_copy(
                src_ref=v_send.at[k, b, pl.ds(c * part_rows, part_rows), :],
                dst_ref=v_recv.at[k, mine(c), :],
                send_sem=vs.at[k, c, d],
                recv_sem=vr.at[k, c, d],
                device_id=device,
                device_id_type=MESH,
            )
            copy.start()
            kept[k].append(copy)

    def keep_rows(k, c):
        v_recv[k, mine(c), :] = v_send[k, me, pl.ds(c * part_rows, part_rows), :]

    part_send[...] = jnp.zeros_like(part_send)
    part_copies = []

    def bias_of(k):
        for copy in green_copies[k]:
            copy.wait_recv()
        partial_of(k)
        part_copies.append(send_part(k))

    def field_of(k):
        for copy in part_copies[k]:
            copy.wait_recv()
        spread_field(k)

    bias_of(0)
    if count > 1:
        green_copies[1] += send_green(1, range(held, planes))
    for k in range(2, count):
        green_copies[k] += send_green(k, hops)
    for k in range(count):
        field_of(k)
        last = k == count - 1
        for c in range(chunks):
            potential_rows(k, c)
            send_rows(k, c, near, near_copies)
            if not last:
                send_rows(k, c, far, far_copies)
            keep_rows(k, c)
            if c == 0 and not last:
                bias_of(k + 1)
        if last:
            for c in range(chunks):
                send_rows(k, c, far, far_copies)

    for k in range(count):
        for degree in range(1, 5):
            def product_rows(base):
                at = pl.ds(pl.multiple_of(base, strip), strip)
                before = walkers_ref[k] if degree == 1 else term[degree % 2]
                product = (-STEP_ROOT / degree) * jnp.dot(
                    v_recv[k, at, :], before, preferred_element_type=jnp.float32
                )
                so_far = walkers_ref[k, at, :].astype(jnp.float32) if degree == 1 else running[at, :]
                if degree == 4:
                    out_ref[k, at, :] = (so_far + product).astype(jnp.bfloat16)
                else:
                    running[at, :] = so_far + product
                    term[(degree + 1) % 2, at, :] = product.astype(jnp.bfloat16)

            if degree == 1:
                for copy in near_copies[k]:
                    copy.wait_recv()
                product_rows(side * strip)
                for copy in far_copies[k]:
                    copy.wait_recv()
                product_rows((1 - side) * strip)
            else:
                product_rows(0)
                product_rows(strip)

    for group in (green_copies, part_copies, near_copies, far_copies):
        for copies in group:
            for copy in copies:
                copy.wait_send()


def per_device(walkers, intersection_inverse, noise_index, cholesky):
    count, orbitals, electrons = walkers.shape
    vectors, rows = cholesky.shape[:2]
    along_wa = lax.axis_size("wa")
    along_col = lax.axis_size("col")
    planes = along_wa * along_col
    if rows % (2 * BLOCK) or planes != SUBLANES or vectors > LANES:
        return exchange_form(walkers, intersection_inverse, noise_index, cholesky)
    blocks = rows // BLOCK
    chunks = 2
    deep, wide = vectors * BLOCK, planes * BLOCK
    vmem = pl.BlockSpec(memory_space=pltpu.VMEM)
    sem = pltpu.SemaphoreType.DMA
    walkers_new, log_weight = pl.pallas_call(
        functools.partial(step_kernel, along_wa, along_col, chunks),
        out_shape=(
            jax.ShapeDtypeStruct(walkers.shape, jnp.bfloat16),
            jax.ShapeDtypeStruct((count,), jnp.float32),
        ),
        in_specs=[pl.BlockSpec(memory_space=pltpu.HBM)] * 4,
        out_specs=(vmem, pl.BlockSpec(memory_space=pltpu.SMEM)),
        scratch_shapes=[
            pltpu.VMEM(walkers.shape, jnp.bfloat16),
            pltpu.VMEM(intersection_inverse.shape, jnp.bfloat16),
            pltpu.VMEM(noise_index.shape, jnp.int32),
            pltpu.VMEM((blocks, vectors, BLOCK, orbitals), jnp.bfloat16),
            pltpu.VMEM((count, orbitals, electrons), jnp.bfloat16),
            pltpu.VMEM((count, planes, rows, electrons), jnp.bfloat16),
            pltpu.VMEM((count, 2, planes, LANES), jnp.float32),
            pltpu.VMEM((count, planes, 2, planes, LANES), jnp.float32),
            pltpu.VMEM((count, planes, rows, orbitals), jnp.bfloat16),
            pltpu.VMEM((count, orbitals, orbitals), jnp.bfloat16),
            pltpu.VMEM((deep, wide), jnp.float32),
            pltpu.VMEM((wide, deep), jnp.bfloat16),
            pltpu.VMEM((2, orbitals, electrons), jnp.bfloat16),
            pltpu.VMEM((orbitals, electrons), jnp.float32),
            sem((3, count)), sem((blocks,)),
            sem((count, planes)), sem((count, planes)),
            sem((count, planes)), sem((count, planes)),
            sem((count, chunks, planes)), sem((count, chunks, planes)),
        ],
        compiler_params=pltpu.CompilerParams(
            collective_id=0, has_side_effects=True, vmem_limit_bytes=52736 * 1024
        ),
    )(walkers, intersection_inverse, noise_index, cholesky)
    return walkers_new, log_weight


def solution(mesh):
    placed = (
        P(("grp", "wa", "col", "row"), None, None),
        P(("grp", "wa", "col", "row"), None, None),
        P(("grp", "wa", "col", "row"), None),
        P(None, ("wa", "col"), None),
    )
    return jax.shard_map(
        per_device,
        mesh=mesh,
        in_specs=placed,
        out_specs=(P(("grp", "wa", "col", "row"), None, None), P(("grp", "wa", "col", "row"))),
        check_vma=False,
    )
```

```python
import functools

import jax
import jax.numpy as jnp
from jax import lax
from jax.experimental import pallas as pl
from jax.experimental.pallas import tpu as pltpu
from jax.sharding import PartitionSpec as P

NOISE_LEVELS = 65536


STEP_ROOT = 0.1
BIAS_CAP = 1.0
ROOT_TWO = 1.4142135623730951


def force_terms(green_tiles, half_tile):
    return jnp.einsum("ksf,gf->ksg", green_tiles, half_tile, preferred_element_type=jnp.float32)


def shift_field(bias_sum, code_block):
    force_bias = jnp.clip(STEP_ROOT * bias_sum, -BIAS_CAP, BIAS_CAP)
    level = (code_block.astype(jnp.float32) + 0.5) / NOISE_LEVELS
    noise = ROOT_TWO * lax.erf_inv(2.0 * level - 1.0)
    shifted = noise - force_bias
    log_step = jnp.sum(shifted * force_bias - 0.5 * force_bias * force_bias, axis=-1)
    return (shifted.astype(jnp.bfloat16), log_step)


def exchange_form(walkers, intersection_inverse, noise_index, cholesky):
    walker_count = walkers.shape[0]
    orbitals = walkers.shape[1]
    electrons = walkers.shape[2]
    vectors = cholesky.shape[0]
    tile_rows = cholesky.shape[1]
    along_wa = lax.axis_size("wa")
    along_col = lax.axis_size("col")
    planes = along_wa * along_col
    green_half = jnp.einsum(
        "kpe,kef->kpf", walkers, intersection_inverse, preferred_element_type=jnp.float32
    ).astype(jnp.bfloat16)
    packed = green_half.reshape(walker_count, planes, tile_rows * electrons)
    half_tile = cholesky[:, :, :electrons].reshape(vectors, tile_rows * electrons)
    partial_sums = force_terms(
        lax.all_to_all(packed, ("wa", "col"), split_axis=1, concat_axis=1, tiled=True), half_tile
    )
    bias_sum = lax.psum(partial_sums, ("wa", "col"))
    gathered = lax.all_gather(noise_index, ("wa", "col"), axis=0, tiled=True)
    gathered = jnp.transpose(gathered.reshape(planes, walker_count, vectors), (1, 0, 2))
    field, log_all = shift_field(bias_sum, gathered)
    log_weight = lax.dynamic_slice_in_dim(log_all, lax.axis_index(("wa", "col")), 1, 1)[:, 0]
    full_tile = cholesky.reshape(vectors, tile_rows * orbitals)
    tiles_out = jnp.einsum(
        "ksg,gf->ksf", field, full_tile, preferred_element_type=jnp.float32
    ).astype(jnp.bfloat16)
    returned = lax.all_to_all(tiles_out, ("wa", "col"), split_axis=1, concat_axis=1, tiled=True)
    potential = returned.reshape(walker_count, orbitals, orbitals)
    running = walkers.astype(jnp.float32)
    factor_term = walkers
    for degree in range(1, 5):
        product = (
            -STEP_ROOT
            / degree
            * jnp.einsum("kpq,kqe->kpe", potential, factor_term, preferred_element_type=jnp.float32)
        )
        running = running + product
        factor_term = product.astype(jnp.bfloat16)
    return (running.astype(jnp.bfloat16), log_weight)


BLOCK = 16
LANES = 128
SPLIT = LANES // 2
SUBLANES = 8
MESH = pl.DeviceIdType.MESH


def step_kernel(
    along_wa, along_col, chunks, pieces,
    walkers_hbm, inverse_hbm, noise_hbm, chol_hbm, out_ref, log_ref,
    walkers_ref, inverse_ref, noise_ref,
    chol, green_send, green_recv, part_send, part_recv, half_send, half_recv, v_send, v_recv, total, spread, term, running,
    in_sem, chol_sem, gs, gr, ps, pr, hs, hr, vs, vr,
):
    planes = along_wa * along_col
    count, orbitals, electrons = walkers_ref.shape
    blocks, vectors = chol.shape[0], chol.shape[1]
    rows = blocks * BLOCK
    wide = planes * BLOCK
    deep = vectors * BLOCK
    me = lax.axis_index("wa") * along_col + lax.axis_index("col")
    half = planes // 2
    hops = range(1, planes)
    near, far = range(1, half), range(half, planes)

    def peer(d):
        b = me
        for bit in (1 << i for i in range(planes.bit_length() - 1)):
            if d & bit:
                b = b + bit * (1 - 2 * lax.rem(me // bit, 2))
        return b, {"wa": b // along_col, "col": lax.rem(b, along_col)}

    loads = [
        pltpu.make_async_copy(chol_hbm.at[:, pl.ds(b * BLOCK, BLOCK), :], chol.at[b], chol_sem.at[b])
        for b in range(blocks)
    ]
    barrier = pltpu.get_barrier_semaphore()
    for d in hops:
        pl.semaphore_signal(barrier, inc=1, device_id=peer(d)[1], device_id_type=MESH)
    inputs = [
        pltpu.make_async_copy(hbm.at[k], ref.at[k], in_sem.at[i, k])
        for k in range(count)
        for i, (hbm, ref) in enumerate(((walkers_hbm, walkers_ref), (inverse_hbm, inverse_ref)))
    ]
    inputs.append(pltpu.make_async_copy(noise_hbm, noise_ref, in_sem.at[2, 0]))
    for load in inputs:
        load.start()

    strip = half * rows

    side = me // half

    def green_of(k, base):
        at = pl.ds(pl.multiple_of(base, strip), strip)
        green_send[k, at, :] = jnp.dot(
            walkers_ref[k, at, :], inverse_ref[k], preferred_element_type=jnp.float32
        ).astype(jnp.bfloat16)

    piece_rows = rows // pieces

    def send_green(k, those):
        for j, d in those:
            b, device = peer(d)
            copy = pltpu.make_async_remote_copy(
                src_ref=green_send.at[k, pl.ds(pl.multiple_of(b * rows + j * piece_rows, BLOCK), piece_rows), :],
                dst_ref=green_recv.at[k, me, pl.ds(j * piece_rows, piece_rows), :],
                send_sem=gs.at[k, d, j],
                recv_sem=gr.at[k, d, j],
                device_id=device,
                device_id_type=MESH,
            )
            copy.start()
            green_copies[k][j].append(copy)

    def keep_green(k):
        green_recv[k, me] = green_send[k, pl.ds(pl.multiple_of(me * rows, rows), rows), :]

    green_copies = [[[] for j in range(pieces)] for k in range(count)]
    across = [(j, d) for j in range(pieces) for d in far]
    beside = [(j, d) for j in range(pieces) for d in near]
    held = len(across) // 2
    for k in range(count):
        for load in inputs[2 * k : 2 * k + 2]:
            load.wait()
        green_of(k, (1 - side) * strip)
        if k == 0:
            pl.semaphore_wait(barrier, planes - 1)
        if k < 2:
            send_green(k, across if k == 0 else across[:held])
        if k == 0:
            for load in loads:
                load.start()
        green_of(k, side * strip)
        if k < 2:
            send_green(k, beside)
        keep_green(k)
    for load in (inputs[-1], *loads):
        load.wait()

    row_in = lax.broadcasted_iota(jnp.int32, (deep, wide), 0) % BLOCK
    col_in = lax.broadcasted_iota(jnp.int32, (deep, wide), 1) % BLOCK
    pick = (
        lax.broadcasted_iota(jnp.int32, (planes, wide), 1) // BLOCK
        == lax.broadcasted_iota(jnp.int32, (planes, wide), 0)
    ).astype(jnp.float32)

    def noise_of(k):
        level = (noise_ref[k : k + 1, :].astype(jnp.float32) + 0.5) / NOISE_LEVELS
        return ROOT_TWO * lax.erf_inv(2.0 * level - 1.0)

    def partial_of(k):
        each_piece = blocks // pieces

        def block_dot(i):
            left = chol[i, :, :, :electrons].reshape(deep, electrons)
            right = green_recv[k, :, i * BLOCK : (i + 1) * BLOCK, :].reshape(wide, electrons)
            return lax.dot_general(left, right, (((1,), (1,)), ((), ())), preferred_element_type=jnp.float32)

        for j in range(pieces):
            for copy in green_copies[k][j]:
                copy.wait_recv()
            summed = block_dot(j * each_piece)
            for i in range(j * each_piece + 1, (j + 1) * each_piece):
                summed = summed + block_dot(i)
            total[...] = summed if j == 0 else total[...] + summed
        kept = jnp.where(row_in == col_in, total[...], 0.0).reshape(vectors, BLOCK, wide).sum(axis=1)
        sums = lax.dot_general(
            pick, kept, (((1,), (1,)), ((), ())),
            preferred_element_type=jnp.float32, precision=lax.Precision.HIGHEST,
        )
        own = lax.broadcasted_iota(jnp.int32, (planes, vectors), 0) == me
        part_send[k, :, :vectors] = sums
        part_send[k, :, SPLIT : SPLIT + vectors] = jnp.where(own, noise_of(k), 0.0)

    def send_part(k):
        copies = []
        for d in near:
            copy = pltpu.make_async_remote_copy(
                src_ref=part_send.at[k],
                dst_ref=part_recv.at[k, me],
                send_sem=ps.at[k, d],
                recv_sem=pr.at[k, d],
                device_id=peer(d)[1],
                device_id_type=MESH,
            )
            copy.start()
            copies.append(copy)
        part_recv[k, me] = part_send[k]
        return copies

    half_copies = [
        pltpu.make_async_remote_copy(
            src_ref=half_send.at[k],
            dst_ref=half_recv.at[k],
            send_sem=hs.at[k],
            recv_sem=hr.at[k],
            device_id=peer(half)[1],
            device_id_type=MESH,
        )
        for k in range(count)
    ]

    def send_half(k):
        for copy in part_copies[k]:
            copy.wait_recv()
        summed = part_recv[k, side * half]
        for a in range(1, half):
            summed = summed + part_recv[k, side * half + a]
        half_send[k] = summed
        half_copies[k].start()

    plane_row = lax.broadcasted_iota(jnp.int32, (planes, LANES), 0)
    vector_lane = lax.broadcasted_iota(jnp.int32, (planes, LANES), 1) < SPLIT

    def spread_field(k):
        both = half_send[k] + half_recv[k]
        bias_sum = jnp.where(vector_lane, both, 0.0)
        noise = jnp.where(vector_lane, pltpu.roll(both, LANES - SPLIT, 1), 0.0)
        force = jnp.clip(STEP_ROOT * bias_sum, -BIAS_CAP, BIAS_CAP)
        shifted = noise - force
        steps = jnp.where(plane_row == me, shifted * force - 0.5 * force * force, 0.0)
        log_ref[k] = jnp.sum(steps)
        field = shifted.astype(jnp.bfloat16)
        tall = (
            lax.broadcasted_iota(jnp.int32, (wide, planes), 0) // BLOCK
            == lax.broadcasted_iota(jnp.int32, (wide, planes), 1)
        ).astype(jnp.float32)
        by_row = jnp.dot(tall, field.astype(jnp.float32), preferred_element_type=jnp.float32)
        out = (
            lax.broadcasted_iota(jnp.int32, (LANES, deep), 1) // BLOCK
            == lax.broadcasted_iota(jnp.int32, (LANES, deep), 0)
        ).astype(jnp.float32).astype(jnp.bfloat16)
        both = jnp.dot(by_row.astype(jnp.bfloat16), out, preferred_element_type=jnp.float32)
        same = (
            lax.broadcasted_iota(jnp.int32, (wide, deep), 0) % BLOCK
            == lax.broadcasted_iota(jnp.int32, (wide, deep), 1) % BLOCK
        )
        spread[...] = jnp.where(same, both, 0.0).astype(jnp.bfloat16)

    each = blocks // chunks
    part_rows = each * BLOCK

    def potential_rows(k, c):
        def body(i, carry):
            b = c * each + i
            tile = jnp.dot(
                spread[...], chol[b].reshape(deep, orbitals), preferred_element_type=jnp.float32
            ).astype(jnp.bfloat16)
            v_send[k, :, pl.ds(pl.multiple_of(b * BLOCK, BLOCK), BLOCK), :] = tile.reshape(
                planes, BLOCK, orbitals
            )
            return carry

        lax.fori_loop(0, each, body, 0)

    def mine(c):
        return pl.ds(pl.multiple_of(me * rows + c * part_rows, BLOCK), part_rows)

    near_copies = [[] for k in range(count)]
    far_copies = [[] for k in range(count)]

    def send_rows(k, c, those, kept):
        for d in those:
            b, device = peer(d)
            copy = pltpu.make_async_remote_copy(
                src_ref=v_send.at[k, b, pl.ds(c * part_rows, part_rows), :],
                dst_ref=v_recv.at[k, mine(c), :],
                send_sem=vs.at[k, c, d],
                recv_sem=vr.at[k, c, d],
                device_id=device,
                device_id_type=MESH,
            )
            copy.start()
            kept[k].append(copy)

    def keep_rows(k, c):
        v_recv[k, mine(c), :] = v_send[k, me, pl.ds(c * part_rows, part_rows), :]

    part_send[...] = jnp.zeros_like(part_send)
    part_copies = []

    def bias_of(k):
        partial_of(k)
        part_copies.append(send_part(k))
        send_half(k)

    def field_of(k):
        half_copies[k].wait_recv()
        spread_field(k)

    bias_of(0)
    if count > 1:
        send_green(1, across[held:])
    for k in range(2, count):
        send_green(k, across + beside)
    for k in range(count):
        field_of(k)
        last = k == count - 1
        for c in range(chunks):
            potential_rows(k, c)
            send_rows(k, c, far, far_copies)
            send_rows(k, c, near, near_copies)
            keep_rows(k, c)
            if c == 0 and not last:
                bias_of(k + 1)

    for k in range(count):
        for degree in range(1, 5):
            def product_rows(base):
                at = pl.ds(pl.multiple_of(base, strip), strip)
                before = walkers_ref[k] if degree == 1 else term[degree % 2]
                product = (-STEP_ROOT / degree) * jnp.dot(
                    v_recv[k, at, :], before, preferred_element_type=jnp.float32
                )
                so_far = walkers_ref[k, at, :].astype(jnp.float32) if degree == 1 else running[at, :]
                if degree == 4:
                    out_ref[k, at, :] = (so_far + product).astype(jnp.bfloat16)
                else:
                    running[at, :] = so_far + product
                    term[(degree + 1) % 2, at, :] = product.astype(jnp.bfloat16)

            if degree == 1:
                for copy in near_copies[k]:
                    copy.wait_recv()
                product_rows(side * strip)
                for copy in far_copies[k]:
                    copy.wait_recv()
                product_rows((1 - side) * strip)
            else:
                product_rows(0)
                product_rows(strip)

    for group in (*green_copies, part_copies, [half_copies], near_copies, far_copies):
        for copies in group:
            for copy in copies:
                copy.wait_send()


def per_device(walkers, intersection_inverse, noise_index, cholesky):
    count, orbitals, electrons = walkers.shape
    vectors, rows = cholesky.shape[:2]
    along_wa = lax.axis_size("wa")
    along_col = lax.axis_size("col")
    planes = along_wa * along_col
    if rows % (2 * BLOCK) or planes != SUBLANES or vectors > SPLIT:
        return exchange_form(walkers, intersection_inverse, noise_index, cholesky)
    blocks = rows // BLOCK
    chunks = 2
    pieces = 2
    deep, wide = vectors * BLOCK, planes * BLOCK
    vmem = pl.BlockSpec(memory_space=pltpu.VMEM)
    sem = pltpu.SemaphoreType.DMA
    walkers_new, log_weight = pl.pallas_call(
        functools.partial(step_kernel, along_wa, along_col, chunks, pieces),
        out_shape=(
            jax.ShapeDtypeStruct(walkers.shape, jnp.bfloat16),
            jax.ShapeDtypeStruct((count,), jnp.float32),
        ),
        in_specs=[pl.BlockSpec(memory_space=pltpu.HBM)] * 4,
        out_specs=(vmem, pl.BlockSpec(memory_space=pltpu.SMEM)),
        scratch_shapes=[
            pltpu.VMEM(walkers.shape, jnp.bfloat16),
            pltpu.VMEM(intersection_inverse.shape, jnp.bfloat16),
            pltpu.VMEM(noise_index.shape, jnp.int32),
            pltpu.VMEM((blocks, vectors, BLOCK, orbitals), jnp.bfloat16),
            pltpu.VMEM((count, orbitals, electrons), jnp.bfloat16),
            pltpu.VMEM((count, planes, rows, electrons), jnp.bfloat16),
            pltpu.VMEM((count, planes, LANES), jnp.float32),
            pltpu.VMEM((count, planes, planes, LANES), jnp.float32),
            pltpu.VMEM((count, planes, LANES), jnp.float32),
            pltpu.VMEM((count, planes, LANES), jnp.float32),
            pltpu.VMEM((count, planes, rows, orbitals), jnp.bfloat16),
            pltpu.VMEM((count, orbitals, orbitals), jnp.bfloat16),
            pltpu.VMEM((deep, wide), jnp.float32),
            pltpu.VMEM((wide, deep), jnp.bfloat16),
            pltpu.VMEM((2, orbitals, electrons), jnp.bfloat16),
            pltpu.VMEM((orbitals, electrons), jnp.float32),
            sem((3, count)), sem((blocks,)),
            sem((count, planes, pieces)), sem((count, planes, pieces)),
            sem((count, planes)), sem((count, planes)), sem((count,)), sem((count,)),
            sem((count, chunks, planes)), sem((count, chunks, planes)),
        ],
        compiler_params=pltpu.CompilerParams(
            collective_id=0, has_side_effects=True, vmem_limit_bytes=52736 * 1024
        ),
    )(walkers, intersection_inverse, noise_index, cholesky)
    return walkers_new, log_weight


def solution(mesh):
    placed = (
        P(("grp", "wa", "col", "row"), None, None),
        P(("grp", "wa", "col", "row"), None, None),
        P(("grp", "wa", "col", "row"), None),
        P(None, ("wa", "col"), None),
    )
    return jax.shard_map(
        per_device,
        mesh=mesh,
        in_specs=placed,
        out_specs=(P(("grp", "wa", "col", "row"), None, None), P(("grp", "wa", "col", "row"))),
        check_vma=False,
    )
```

```python
import functools

import jax
import jax.numpy as jnp
from jax import lax
from jax.experimental import pallas as pl
from jax.experimental.pallas import tpu as pltpu
from jax.sharding import PartitionSpec as P

NOISE_LEVELS = 65536


STEP_ROOT = 0.1
BIAS_CAP = 1.0
ROOT_TWO = 1.4142135623730951


def force_terms(green_tiles, half_tile):
    return jnp.einsum("ksf,gf->ksg", green_tiles, half_tile, preferred_element_type=jnp.float32)


def shift_field(bias_sum, code_block):
    force_bias = jnp.clip(STEP_ROOT * bias_sum, -BIAS_CAP, BIAS_CAP)
    level = (code_block.astype(jnp.float32) + 0.5) / NOISE_LEVELS
    noise = ROOT_TWO * lax.erf_inv(2.0 * level - 1.0)
    shifted = noise - force_bias
    log_step = jnp.sum(shifted * force_bias - 0.5 * force_bias * force_bias, axis=-1)
    return (shifted.astype(jnp.bfloat16), log_step)


def exchange_form(walkers, intersection_inverse, noise_index, cholesky):
    walker_count = walkers.shape[0]
    orbitals = walkers.shape[1]
    electrons = walkers.shape[2]
    vectors = cholesky.shape[0]
    tile_rows = cholesky.shape[1]
    along_wa = lax.axis_size("wa")
    along_col = lax.axis_size("col")
    planes = along_wa * along_col
    green_half = jnp.einsum(
        "kpe,kef->kpf", walkers, intersection_inverse, preferred_element_type=jnp.float32
    ).astype(jnp.bfloat16)
    packed = green_half.reshape(walker_count, planes, tile_rows * electrons)
    half_tile = cholesky[:, :, :electrons].reshape(vectors, tile_rows * electrons)
    partial_sums = force_terms(
        lax.all_to_all(packed, ("wa", "col"), split_axis=1, concat_axis=1, tiled=True), half_tile
    )
    bias_sum = lax.psum(partial_sums, ("wa", "col"))
    gathered = lax.all_gather(noise_index, ("wa", "col"), axis=0, tiled=True)
    gathered = jnp.transpose(gathered.reshape(planes, walker_count, vectors), (1, 0, 2))
    field, log_all = shift_field(bias_sum, gathered)
    log_weight = lax.dynamic_slice_in_dim(log_all, lax.axis_index(("wa", "col")), 1, 1)[:, 0]
    full_tile = cholesky.reshape(vectors, tile_rows * orbitals)
    tiles_out = jnp.einsum(
        "ksg,gf->ksf", field, full_tile, preferred_element_type=jnp.float32
    ).astype(jnp.bfloat16)
    returned = lax.all_to_all(tiles_out, ("wa", "col"), split_axis=1, concat_axis=1, tiled=True)
    potential = returned.reshape(walker_count, orbitals, orbitals)
    running = walkers.astype(jnp.float32)
    factor_term = walkers
    for degree in range(1, 5):
        product = (
            -STEP_ROOT
            / degree
            * jnp.einsum("kpq,kqe->kpe", potential, factor_term, preferred_element_type=jnp.float32)
        )
        running = running + product
        factor_term = product.astype(jnp.bfloat16)
    return (running.astype(jnp.bfloat16), log_weight)


BLOCK = 16
LANES = 128
SPLIT = LANES // 2
SUBLANES = 8
MESH = pl.DeviceIdType.MESH


def step_kernel(
    along_wa, along_col, chunks, pieces,
    walkers_hbm, inverse_hbm, noise_hbm, chol_hbm, out_ref, log_ref,
    walkers_ref, inverse_ref, noise_ref,
    chol, green_send, green_recv, part_send, part_recv, half_send, half_recv, v_send, v_recv, total, spread, term, running,
    late, series, tied, late_sum, in_sem, chol_sem, gs, gr, ps, pr, hs, hr, vs, vr,
):
    planes = along_wa * along_col
    count, orbitals, electrons = walkers_ref.shape
    blocks, vectors = chol.shape[0], chol.shape[1]
    rows = blocks * BLOCK
    wide = planes * BLOCK
    deep = vectors * BLOCK
    me = lax.axis_index("wa") * along_col + lax.axis_index("col")
    half = planes // 2
    hops = range(1, planes)
    near, far = range(1, half), range(half, planes)

    def peer(d):
        b = me
        for bit in (1 << i for i in range(planes.bit_length() - 1)):
            if d & bit:
                b = b + bit * (1 - 2 * lax.rem(me // bit, 2))
        return b, {"wa": b // along_col, "col": lax.rem(b, along_col)}

    loads = [
        pltpu.make_async_copy(chol_hbm.at[:, pl.ds(b * BLOCK, BLOCK), :], chol.at[b], chol_sem.at[b])
        for b in range(blocks)
    ]
    barrier = pltpu.get_barrier_semaphore()
    for d in hops:
        pl.semaphore_signal(barrier, inc=1, device_id=peer(d)[1], device_id_type=MESH)
    inputs = [
        pltpu.make_async_copy(hbm.at[k], ref.at[k], in_sem.at[i, k])
        for k in range(count)
        for i, (hbm, ref) in enumerate(((walkers_hbm, walkers_ref), (inverse_hbm, inverse_ref)))
    ]
    inputs.append(pltpu.make_async_copy(noise_hbm, noise_ref, in_sem.at[2, 0]))
    for load in inputs:
        load.start()

    strip = half * rows

    side = me // half

    def green_of(k, base):
        at = pl.ds(pl.multiple_of(base, strip), strip)
        green_send[k, at, :] = jnp.dot(
            walkers_ref[k, at, :], inverse_ref[k], preferred_element_type=jnp.float32
        ).astype(jnp.bfloat16)

    piece_rows = rows // pieces

    def send_green(k, those):
        for j, d in those:
            b, device = peer(d)
            copy = pltpu.make_async_remote_copy(
                src_ref=green_send.at[k, pl.ds(pl.multiple_of(b * rows + j * piece_rows, BLOCK), piece_rows), :],
                dst_ref=green_recv.at[k, me, pl.ds(j * piece_rows, piece_rows), :],
                send_sem=gs.at[k, d, j],
                recv_sem=gr.at[k, d, j],
                device_id=device,
                device_id_type=MESH,
            )
            copy.start()
            green_copies[k][j].append(copy)

    def keep_green(k):
        green_recv[k, me] = green_send[k, pl.ds(pl.multiple_of(me * rows, rows), rows), :]

    green_copies = [[[] for j in range(pieces)] for k in range(count)]
    across = [(j, d) for j in range(pieces) for d in far]
    beside = [(j, d) for j in range(pieces) for d in near]
    held = len(across) // 2
    for k in range(count):
        for load in inputs[2 * k : 2 * k + 2]:
            load.wait()
        green_of(k, (1 - side) * strip)
        if k == 0:
            pl.semaphore_wait(barrier, planes - 1)
        if k < 2:
            send_green(k, across if k == 0 else across[:held])
        if k == 0:
            for load in loads:
                load.start()
        green_of(k, side * strip)
        if k < 2:
            send_green(k, beside)
        keep_green(k)
    for load in (inputs[-1], *loads):
        load.wait()

    row_in = lax.broadcasted_iota(jnp.int32, (deep, wide), 0) % BLOCK
    col_in = lax.broadcasted_iota(jnp.int32, (deep, wide), 1) % BLOCK
    pick = (
        lax.broadcasted_iota(jnp.int32, (planes, wide), 1) // BLOCK
        == lax.broadcasted_iota(jnp.int32, (planes, wide), 0)
    ).astype(jnp.float32)

    def noise_of(k):
        level = (noise_ref[k : k + 1, :].astype(jnp.float32) + 0.5) / NOISE_LEVELS
        return ROOT_TWO * lax.erf_inv(2.0 * level - 1.0)

    def partial_of(k):
        each_piece = blocks // pieces

        def block_dot(i):
            left = chol[i, :, :, :electrons].reshape(deep, electrons)
            right = green_recv[k, :, i * BLOCK : (i + 1) * BLOCK, :].reshape(wide, electrons)
            return lax.dot_general(left, right, (((1,), (1,)), ((), ())), preferred_element_type=jnp.float32)

        for j in range(pieces):
            for copy in green_copies[k][j]:
                copy.wait_recv()
            summed = block_dot(j * each_piece)
            for i in range(j * each_piece + 1, (j + 1) * each_piece):
                summed = summed + block_dot(i)
            total[...] = summed if j == 0 else total[...] + summed
        kept = jnp.where(row_in == col_in, total[...], 0.0).reshape(vectors, BLOCK, wide).sum(axis=1)
        sums = lax.dot_general(
            pick, kept, (((1,), (1,)), ((), ())),
            preferred_element_type=jnp.float32, precision=lax.Precision.HIGHEST,
        )
        own = lax.broadcasted_iota(jnp.int32, (planes, vectors), 0) == me
        part_send[k, :, :vectors] = sums
        part_send[k, :, SPLIT : SPLIT + vectors] = jnp.where(own, noise_of(k), 0.0)

    def send_part(k):
        copies = []
        for d in near:
            copy = pltpu.make_async_remote_copy(
                src_ref=part_send.at[k],
                dst_ref=part_recv.at[k, me],
                send_sem=ps.at[k, d],
                recv_sem=pr.at[k, d],
                device_id=peer(d)[1],
                device_id_type=MESH,
            )
            copy.start()
            copies.append(copy)
        part_recv[k, me] = part_send[k]
        return copies

    half_copies = [
        pltpu.make_async_remote_copy(
            src_ref=half_send.at[k],
            dst_ref=half_recv.at[k],
            send_sem=hs.at[k],
            recv_sem=hr.at[k],
            device_id=peer(half)[1],
            device_id_type=MESH,
        )
        for k in range(count)
    ]

    def send_half(k):
        for copy in part_copies[k]:
            copy.wait_recv()
        summed = part_recv[k, side * half]
        for a in range(1, half):
            summed = summed + part_recv[k, side * half + a]
        half_send[k] = summed
        half_copies[k].start()

    plane_row = lax.broadcasted_iota(jnp.int32, (planes, LANES), 0)
    vector_lane = lax.broadcasted_iota(jnp.int32, (planes, LANES), 1) < SPLIT

    def spread_field(k):
        both = half_send[k] + half_recv[k]
        bias_sum = jnp.where(vector_lane, both, 0.0)
        noise = jnp.where(vector_lane, pltpu.roll(both, LANES - SPLIT, 1), 0.0)
        force = jnp.clip(STEP_ROOT * bias_sum, -BIAS_CAP, BIAS_CAP)
        shifted = noise - force
        steps = jnp.where(plane_row == me, shifted * force - 0.5 * force * force, 0.0)
        log_ref[k] = jnp.sum(steps)
        field = shifted.astype(jnp.bfloat16)
        tall = (
            lax.broadcasted_iota(jnp.int32, (wide, planes), 0) // BLOCK
            == lax.broadcasted_iota(jnp.int32, (wide, planes), 1)
        ).astype(jnp.float32)
        by_row = jnp.dot(tall, field.astype(jnp.float32), preferred_element_type=jnp.float32)
        out = (
            lax.broadcasted_iota(jnp.int32, (LANES, deep), 1) // BLOCK
            == lax.broadcasted_iota(jnp.int32, (LANES, deep), 0)
        ).astype(jnp.float32).astype(jnp.bfloat16)
        both = jnp.dot(by_row.astype(jnp.bfloat16), out, preferred_element_type=jnp.float32)
        same = (
            lax.broadcasted_iota(jnp.int32, (wide, deep), 0) % BLOCK
            == lax.broadcasted_iota(jnp.int32, (wide, deep), 1) % BLOCK
        )
        spread[...] = jnp.where(same, both, 0.0).astype(jnp.bfloat16)

    each = blocks // chunks
    part_rows = each * BLOCK

    def potential_rows(k, c):
        def body(i, carry):
            b = c * each + i
            tile = jnp.dot(
                spread[...], chol[b].reshape(deep, orbitals), preferred_element_type=jnp.float32
            ).astype(jnp.bfloat16)
            v_send[k, :, pl.ds(pl.multiple_of(b * BLOCK, BLOCK), BLOCK), :] = tile.reshape(
                planes, BLOCK, orbitals
            )
            return carry

        lax.fori_loop(0, each, body, 0)

    def mine(c):
        return pl.ds(pl.multiple_of(me * rows + c * part_rows, BLOCK), part_rows)

    final = count - 1
    apart = planes - 1
    late_at = pl.ds(pl.multiple_of(peer(apart)[0] * rows, rows), rows)
    v_recv[final, late_at, :] = jnp.zeros((rows, orbitals), jnp.bfloat16)
    late_copy = pltpu.make_async_remote_copy(
        src_ref=v_send.at[final, peer(apart)[0]],
        dst_ref=late,
        send_sem=vs.at[final, 0, apart],
        recv_sem=vr.at[final, 0, apart],
        device_id=peer(apart)[1],
        device_id_type=MESH,
    )
    near_copies = [[] for k in range(count)]
    far_copies = [[] for k in range(count)]

    def send_rows(k, c, those, kept):
        for d in those:
            b, device = peer(d)
            copy = pltpu.make_async_remote_copy(
                src_ref=v_send.at[k, b, pl.ds(c * part_rows, part_rows), :],
                dst_ref=v_recv.at[k, mine(c), :],
                send_sem=vs.at[k, c, d],
                recv_sem=vr.at[k, c, d],
                device_id=device,
                device_id_type=MESH,
            )
            copy.start()
            kept[k].append(copy)

    def keep_rows(k, c):
        v_recv[k, mine(c), :] = v_send[k, me, pl.ds(c * part_rows, part_rows), :]

    part_send[...] = jnp.zeros_like(part_send)
    part_copies = []

    def bias_of(k):
        partial_of(k)
        part_copies.append(send_part(k))
        send_half(k)

    def field_of(k):
        half_copies[k].wait_recv()
        spread_field(k)

    bias_of(0)
    if count > 1:
        send_green(1, across[held:])
    for k in range(2, count):
        send_green(k, across + beside)
    for k in range(count):
        field_of(k)
        last = k == count - 1
        for c in range(chunks):
            potential_rows(k, c)
            send_rows(k, c, range(half, apart) if last else far, far_copies)
            send_rows(k, c, near, near_copies)
            keep_rows(k, c)
            if c == 0 and not last:
                bias_of(k + 1)
        if last:
            late_copy.start()

    for k in range(final):
        for degree in range(1, 5):
            def product_rows(base):
                at = pl.ds(pl.multiple_of(base, strip), strip)
                before = walkers_ref[k] if degree == 1 else term[degree % 2]
                product = (-STEP_ROOT / degree) * jnp.dot(
                    v_recv[k, at, :], before, preferred_element_type=jnp.float32
                )
                so_far = walkers_ref[k, at, :].astype(jnp.float32) if degree == 1 else running[at, :]
                if degree == 4:
                    out_ref[k, at, :] = (so_far + product).astype(jnp.bfloat16)
                else:
                    running[at, :] = so_far + product
                    term[(degree + 1) % 2, at, :] = product.astype(jnp.bfloat16)

            if degree == 1:
                for copy in near_copies[k]:
                    copy.wait_recv()
                product_rows(side * strip)
                for copy in far_copies[k]:
                    copy.wait_recv()
                product_rows((1 - side) * strip)
            else:
                product_rows(0)
                product_rows(strip)

    for copy in (*near_copies[final], *far_copies[final]):
        copy.wait_recv()
    scale = [-STEP_ROOT / degree for degree in range(1, 5)]
    halves = [slice(0, strip), slice(strip, 2 * strip)]
    for degree in range(1, 5):
        before = walkers_ref[final] if degree == 1 else series[degree - 2]
        for at in halves:
            product = scale[degree - 1] * jnp.dot(v_recv[final, at, :], before, preferred_element_type=jnp.float32)
            so_far = walkers_ref[final, at, :].astype(jnp.float32) if degree == 1 else running[at, :]
            running[at, :] = so_far + product
            if degree < 4:
                series[degree - 1, at, :] = product.astype(jnp.bfloat16)
    tied[:, :rows] = v_recv[final, :, late_at]
    for power in range(1, 3):
        before = tied[:, (power - 1) * rows : power * rows]
        for at in halves:
            tied[at, power * rows : (power + 1) * rows] = jnp.dot(
                v_recv[final, at, :], before, preferred_element_type=jnp.float32
            ).astype(jnp.bfloat16)

    def times(left, right):
        return jnp.dot(left, right, preferred_element_type=jnp.float32)

    late_copy.wait_recv()
    late_rows = late[...]
    own = late[:, late_at]
    first = scale[0] * times(late_rows, walkers_ref[final])
    term_1 = first.astype(jnp.bfloat16)
    second = scale[1] * (times(late_rows, series[0]) + times(own, term_1))
    term_2 = second.astype(jnp.bfloat16)
    back = times(late_rows, tied[:, : 2 * rows]).astype(jnp.bfloat16)
    third = scale[2] * (
        times(late_rows, series[1]) + scale[1] * times(back[:, :rows], term_1) + times(own, term_2)
    )
    term_3 = third.astype(jnp.bfloat16)
    fourth = scale[3] * (
        times(late_rows, series[2])
        + scale[2] * (scale[1] * times(back[:, rows:], term_1) + times(back[:, :rows], term_2))
        + times(own, term_3)
    )
    late_sum[:rows] = (scale[1] * first + scale[2] * second + scale[3] * third).astype(jnp.bfloat16)
    late_sum[rows : 2 * rows] = (scale[2] * (scale[1] * first + scale[3] * second)).astype(jnp.bfloat16)
    late_sum[2 * rows :] = (scale[3] * scale[2] * scale[1] * first).astype(jnp.bfloat16)
    for at in halves:
        out_ref[final, at, :] = (running[at, :] + times(tied[at, :], late_sum[...])).astype(jnp.bfloat16)
    out_ref[final, late_at, :] = (running[late_at, :] + first + second + third + fourth).astype(jnp.bfloat16)

    for group in (*green_copies, part_copies, [half_copies], near_copies, far_copies, [[late_copy]]):
        for copies in group:
            for copy in copies:
                copy.wait_send()


def per_device(walkers, intersection_inverse, noise_index, cholesky):
    count, orbitals, electrons = walkers.shape
    vectors, rows = cholesky.shape[:2]
    along_wa = lax.axis_size("wa")
    along_col = lax.axis_size("col")
    planes = along_wa * along_col
    if rows % LANES or planes != SUBLANES or vectors > SPLIT:
        return exchange_form(walkers, intersection_inverse, noise_index, cholesky)
    blocks = rows // BLOCK
    chunks = 2
    pieces = 2
    deep, wide = vectors * BLOCK, planes * BLOCK
    vmem = pl.BlockSpec(memory_space=pltpu.VMEM)
    sem = pltpu.SemaphoreType.DMA
    walkers_new, log_weight = pl.pallas_call(
        functools.partial(step_kernel, along_wa, along_col, chunks, pieces),
        out_shape=(
            jax.ShapeDtypeStruct(walkers.shape, jnp.bfloat16),
            jax.ShapeDtypeStruct((count,), jnp.float32),
        ),
        in_specs=[pl.BlockSpec(memory_space=pltpu.HBM)] * 4,
        out_specs=(vmem, pl.BlockSpec(memory_space=pltpu.SMEM)),
        scratch_shapes=[
            pltpu.VMEM(walkers.shape, jnp.bfloat16),
            pltpu.VMEM(intersection_inverse.shape, jnp.bfloat16),
            pltpu.VMEM(noise_index.shape, jnp.int32),
            pltpu.VMEM((blocks, vectors, BLOCK, orbitals), jnp.bfloat16),
            pltpu.VMEM((count, orbitals, electrons), jnp.bfloat16),
            pltpu.VMEM((count, planes, rows, electrons), jnp.bfloat16),
            pltpu.VMEM((count, planes, LANES), jnp.float32),
            pltpu.VMEM((count, planes, planes, LANES), jnp.float32),
            pltpu.VMEM((count, planes, LANES), jnp.float32),
            pltpu.VMEM((count, planes, LANES), jnp.float32),
            pltpu.VMEM((count, planes, rows, orbitals), jnp.bfloat16),
            pltpu.VMEM((count, orbitals, orbitals), jnp.bfloat16),
            pltpu.VMEM((deep, wide), jnp.float32),
            pltpu.VMEM((wide, deep), jnp.bfloat16),
            pltpu.VMEM((2, orbitals, electrons), jnp.bfloat16),
            pltpu.VMEM((orbitals, electrons), jnp.float32),
            pltpu.VMEM((rows, orbitals), jnp.bfloat16),
            pltpu.VMEM((3, orbitals, electrons), jnp.bfloat16),
            pltpu.VMEM((orbitals, 3 * rows), jnp.bfloat16),
            pltpu.VMEM((3 * rows, electrons), jnp.bfloat16),
            sem((3, count)), sem((blocks,)),
            sem((count, planes, pieces)), sem((count, planes, pieces)),
            sem((count, planes)), sem((count, planes)), sem((count,)), sem((count,)),
            sem((count, chunks, planes)), sem((count, chunks, planes)),
        ],
        compiler_params=pltpu.CompilerParams(
            collective_id=0, has_side_effects=True, vmem_limit_bytes=52736 * 1024
        ),
    )(walkers, intersection_inverse, noise_index, cholesky)
    return walkers_new, log_weight


def solution(mesh):
    placed = (
        P(("grp", "wa", "col", "row"), None, None),
        P(("grp", "wa", "col", "row"), None, None),
        P(("grp", "wa", "col", "row"), None),
        P(None, ("wa", "col"), None),
    )
    return jax.shard_map(
        per_device,
        mesh=mesh,
        in_specs=placed,
        out_specs=(P(("grp", "wa", "col", "row"), None, None), P(("grp", "wa", "col", "row"))),
        check_vma=False,
    )
```

```python
import functools

import jax
import jax.numpy as jnp
from jax import lax
from jax.experimental import pallas as pl
from jax.experimental.pallas import tpu as pltpu
from jax.sharding import PartitionSpec as P

NOISE_LEVELS = 65536


STEP_ROOT = 0.1
BIAS_CAP = 1.0
ROOT_TWO = 1.4142135623730951


def force_terms(green_tiles, half_tile):
    return jnp.einsum("ksf,gf->ksg", green_tiles, half_tile, preferred_element_type=jnp.float32)


def shift_field(bias_sum, code_block):
    force_bias = jnp.clip(STEP_ROOT * bias_sum, -BIAS_CAP, BIAS_CAP)
    level = (code_block.astype(jnp.float32) + 0.5) / NOISE_LEVELS
    noise = ROOT_TWO * lax.erf_inv(2.0 * level - 1.0)
    shifted = noise - force_bias
    log_step = jnp.sum(shifted * force_bias - 0.5 * force_bias * force_bias, axis=-1)
    return (shifted.astype(jnp.bfloat16), log_step)


def exchange_form(walkers, intersection_inverse, noise_index, cholesky):
    walker_count = walkers.shape[0]
    orbitals = walkers.shape[1]
    electrons = walkers.shape[2]
    vectors = cholesky.shape[0]
    tile_rows = cholesky.shape[1]
    along_wa = lax.axis_size("wa")
    along_col = lax.axis_size("col")
    planes = along_wa * along_col
    green_half = jnp.einsum(
        "kpe,kef->kpf", walkers, intersection_inverse, preferred_element_type=jnp.float32
    ).astype(jnp.bfloat16)
    packed = green_half.reshape(walker_count, planes, tile_rows * electrons)
    half_tile = cholesky[:, :, :electrons].reshape(vectors, tile_rows * electrons)
    partial_sums = force_terms(
        lax.all_to_all(packed, ("wa", "col"), split_axis=1, concat_axis=1, tiled=True), half_tile
    )
    bias_sum = lax.psum(partial_sums, ("wa", "col"))
    gathered = lax.all_gather(noise_index, ("wa", "col"), axis=0, tiled=True)
    gathered = jnp.transpose(gathered.reshape(planes, walker_count, vectors), (1, 0, 2))
    field, log_all = shift_field(bias_sum, gathered)
    log_weight = lax.dynamic_slice_in_dim(log_all, lax.axis_index(("wa", "col")), 1, 1)[:, 0]
    full_tile = cholesky.reshape(vectors, tile_rows * orbitals)
    tiles_out = jnp.einsum(
        "ksg,gf->ksf", field, full_tile, preferred_element_type=jnp.float32
    ).astype(jnp.bfloat16)
    returned = lax.all_to_all(tiles_out, ("wa", "col"), split_axis=1, concat_axis=1, tiled=True)
    potential = returned.reshape(walker_count, orbitals, orbitals)
    running = walkers.astype(jnp.float32)
    factor_term = walkers
    for degree in range(1, 5):
        product = (
            -STEP_ROOT
            / degree
            * jnp.einsum("kpq,kqe->kpe", potential, factor_term, preferred_element_type=jnp.float32)
        )
        running = running + product
        factor_term = product.astype(jnp.bfloat16)
    return (running.astype(jnp.bfloat16), log_weight)


BLOCK = 16
LANES = 128
SPLIT = LANES // 2
SUBLANES = 8
MESH = pl.DeviceIdType.MESH


def step_kernel(
    along_wa, along_col, chunks, pieces,
    walkers_hbm, inverse_hbm, noise_hbm, chol_hbm, out_ref, log_ref,
    walkers_ref, inverse_ref, noise_ref,
    chol, green_send, green_recv, part_send, part_recv, half_send, half_recv, v_send, v_recv, total, spread, term, running,
    late, series, tied, late_sum, in_sem, chol_sem, gs, gr, ps, pr, hs, hr, vs, vr,
):
    planes = along_wa * along_col
    count, orbitals, electrons = walkers_ref.shape
    blocks, vectors = chol.shape[0], chol.shape[1]
    rows = blocks * BLOCK
    wide = planes * BLOCK
    deep = vectors * BLOCK
    me = lax.axis_index("wa") * along_col + lax.axis_index("col")
    half = planes // 2
    hops = range(1, planes)
    near, far = range(1, half), range(half, planes)

    def peer(d):
        b = me
        for bit in (1 << i for i in range(planes.bit_length() - 1)):
            if d & bit:
                b = b + bit * (1 - 2 * lax.rem(me // bit, 2))
        return b, {"wa": b // along_col, "col": lax.rem(b, along_col)}

    loads = [
        pltpu.make_async_copy(chol_hbm.at[:, pl.ds(b * BLOCK, BLOCK), :], chol.at[b], chol_sem.at[b])
        for b in range(blocks)
    ]
    barrier = pltpu.get_barrier_semaphore()
    for d in hops:
        pl.semaphore_signal(barrier, inc=1, device_id=peer(d)[1], device_id_type=MESH)
    inputs = [
        pltpu.make_async_copy(hbm.at[k], ref.at[k], in_sem.at[i, k])
        for k in range(count)
        for i, (hbm, ref) in enumerate(((walkers_hbm, walkers_ref), (inverse_hbm, inverse_ref)))
    ]
    inputs.append(pltpu.make_async_copy(noise_hbm, noise_ref, in_sem.at[2, 0]))
    for load in inputs:
        load.start()

    strip = half * rows

    side = me // half

    def green_of(k, base):
        at = pl.ds(pl.multiple_of(base, strip), strip)
        green_send[k, at, :] = jnp.dot(
            walkers_ref[k, at, :], inverse_ref[k], preferred_element_type=jnp.float32
        ).astype(jnp.bfloat16)

    piece_rows = rows // pieces

    def send_green(k, those):
        for j, d in those:
            b, device = peer(d)
            copy = pltpu.make_async_remote_copy(
                src_ref=green_send.at[k, pl.ds(pl.multiple_of(b * rows + j * piece_rows, BLOCK), piece_rows), :],
                dst_ref=green_recv.at[k, me, pl.ds(j * piece_rows, piece_rows), :],
                send_sem=gs.at[k, d, j],
                recv_sem=gr.at[k, d, j],
                device_id=device,
                device_id_type=MESH,
            )
            copy.start()
            green_copies[k][j].append(copy)

    def keep_green(k):
        green_recv[k, me] = green_send[k, pl.ds(pl.multiple_of(me * rows, rows), rows), :]

    green_copies = [[[] for j in range(pieces)] for k in range(count)]
    across = [(j, d) for j in range(pieces) for d in far]
    beside = [(j, d) for j in range(pieces) for d in near]
    held = len(across) // 2 + 1
    for k in range(count):
        for load in inputs[2 * k : 2 * k + 2]:
            load.wait()
        green_of(k, (1 - side) * strip)
        if k == 0:
            pl.semaphore_wait(barrier, planes - 1)
        if k < 2:
            send_green(k, across if k == 0 else across[:held])
        if k == 0:
            for load in loads:
                load.start()
        green_of(k, side * strip)
        if k < 2:
            send_green(k, beside)
        keep_green(k)
    for load in (inputs[-1], *loads):
        load.wait()

    row_in = lax.broadcasted_iota(jnp.int32, (deep, wide), 0) % BLOCK
    col_in = lax.broadcasted_iota(jnp.int32, (deep, wide), 1) % BLOCK
    pick = (
        lax.broadcasted_iota(jnp.int32, (planes, wide), 1) // BLOCK
        == lax.broadcasted_iota(jnp.int32, (planes, wide), 0)
    ).astype(jnp.float32)

    def noise_of(k):
        level = (noise_ref[k : k + 1, :].astype(jnp.float32) + 0.5) / NOISE_LEVELS
        return ROOT_TWO * lax.erf_inv(2.0 * level - 1.0)

    def partial_of(k):
        each_piece = blocks // pieces

        def block_dot(i):
            left = chol[i, :, :, :electrons].reshape(deep, electrons)
            right = green_recv[k, :, i * BLOCK : (i + 1) * BLOCK, :].reshape(wide, electrons)
            return lax.dot_general(left, right, (((1,), (1,)), ((), ())), preferred_element_type=jnp.float32)

        for j in range(pieces):
            for copy in green_copies[k][j]:
                copy.wait_recv()
            summed = block_dot(j * each_piece)
            for i in range(j * each_piece + 1, (j + 1) * each_piece):
                summed = summed + block_dot(i)
            total[...] = summed if j == 0 else total[...] + summed
        kept = jnp.where(row_in == col_in, total[...], 0.0).reshape(vectors, BLOCK, wide).sum(axis=1)
        sums = lax.dot_general(
            pick, kept, (((1,), (1,)), ((), ())),
            preferred_element_type=jnp.float32, precision=lax.Precision.HIGHEST,
        )
        own = lax.broadcasted_iota(jnp.int32, (planes, vectors), 0) == me
        part_send[k, :, :vectors] = sums
        part_send[k, :, SPLIT : SPLIT + vectors] = jnp.where(own, noise_of(k), 0.0)

    def send_part(k):
        copies = []
        for d in near:
            copy = pltpu.make_async_remote_copy(
                src_ref=part_send.at[k],
                dst_ref=part_recv.at[k, me],
                send_sem=ps.at[k, d],
                recv_sem=pr.at[k, d],
                device_id=peer(d)[1],
                device_id_type=MESH,
            )
            copy.start()
            copies.append(copy)
        part_recv[k, me] = part_send[k]
        return copies

    half_copies = [
        pltpu.make_async_remote_copy(
            src_ref=half_send.at[k],
            dst_ref=half_recv.at[k],
            send_sem=hs.at[k],
            recv_sem=hr.at[k],
            device_id=peer(half)[1],
            device_id_type=MESH,
        )
        for k in range(count)
    ]

    def send_half(k):
        for copy in part_copies[k]:
            copy.wait_recv()
        summed = part_recv[k, side * half]
        for a in range(1, half):
            summed = summed + part_recv[k, side * half + a]
        half_send[k] = summed
        half_copies[k].start()

    plane_row = lax.broadcasted_iota(jnp.int32, (planes, LANES), 0)
    vector_lane = lax.broadcasted_iota(jnp.int32, (planes, LANES), 1) < SPLIT

    def spread_field(k):
        both = half_send[k] + half_recv[k]
        bias_sum = jnp.where(vector_lane, both, 0.0)
        noise = jnp.where(vector_lane, pltpu.roll(both, LANES - SPLIT, 1), 0.0)
        force = jnp.clip(STEP_ROOT * bias_sum, -BIAS_CAP, BIAS_CAP)
        shifted = noise - force
        steps = jnp.where(plane_row == me, shifted * force - 0.5 * force * force, 0.0)
        log_ref[k] = jnp.sum(steps)
        field = shifted.astype(jnp.bfloat16)
        tall = (
            lax.broadcasted_iota(jnp.int32, (wide, planes), 0) // BLOCK
            == lax.broadcasted_iota(jnp.int32, (wide, planes), 1)
        ).astype(jnp.float32)
        by_row = jnp.dot(tall, field.astype(jnp.float32), preferred_element_type=jnp.float32)
        out = (
            lax.broadcasted_iota(jnp.int32, (LANES, deep), 1) // BLOCK
            == lax.broadcasted_iota(jnp.int32, (LANES, deep), 0)
        ).astype(jnp.float32).astype(jnp.bfloat16)
        both = jnp.dot(by_row.astype(jnp.bfloat16), out, preferred_element_type=jnp.float32)
        same = (
            lax.broadcasted_iota(jnp.int32, (wide, deep), 0) % BLOCK
            == lax.broadcasted_iota(jnp.int32, (wide, deep), 1) % BLOCK
        )
        spread[...] = jnp.where(same, both, 0.0).astype(jnp.bfloat16)

    each = blocks // chunks
    part_rows = each * BLOCK

    def potential_rows(k, c):
        def body(i, carry):
            b = c * each + i
            tile = jnp.dot(
                spread[...], chol[b].reshape(deep, orbitals), preferred_element_type=jnp.float32
            ).astype(jnp.bfloat16)
            v_send[k, :, pl.ds(pl.multiple_of(b * BLOCK, BLOCK), BLOCK), :] = tile.reshape(
                planes, BLOCK, orbitals
            )
            return carry

        lax.fori_loop(0, each, body, 0)

    def mine(c):
        return pl.ds(pl.multiple_of(me * rows + c * part_rows, BLOCK), part_rows)

    final = count - 1
    apart = planes - 1
    late_at = pl.ds(pl.multiple_of(peer(apart)[0] * rows, rows), rows)
    v_recv[final, late_at, :] = jnp.zeros((rows, orbitals), jnp.bfloat16)
    late_copy = pltpu.make_async_remote_copy(
        src_ref=v_send.at[final, peer(apart)[0]],
        dst_ref=late,
        send_sem=vs.at[final, 0, apart],
        recv_sem=vr.at[final, 0, apart],
        device_id=peer(apart)[1],
        device_id_type=MESH,
    )
    near_copies = [[] for k in range(count)]
    far_copies = [[] for k in range(count)]

    def send_rows(k, c, those, kept):
        for d in those:
            b, device = peer(d)
            copy = pltpu.make_async_remote_copy(
                src_ref=v_send.at[k, b, pl.ds(c * part_rows, part_rows), :],
                dst_ref=v_recv.at[k, mine(c), :],
                send_sem=vs.at[k, c, d],
                recv_sem=vr.at[k, c, d],
                device_id=device,
                device_id_type=MESH,
            )
            copy.start()
            kept[k].append(copy)

    def keep_rows(k, c):
        v_recv[k, mine(c), :] = v_send[k, me, pl.ds(c * part_rows, part_rows), :]

    part_send[...] = jnp.zeros_like(part_send)
    part_copies = []

    def bias_of(k):
        partial_of(k)
        part_copies.append(send_part(k))
        send_half(k)

    def field_of(k):
        half_copies[k].wait_recv()
        spread_field(k)

    bias_of(0)
    if count > 1:
        send_green(1, across[held:])
    for k in range(2, count):
        send_green(k, across + beside)
    for k in range(count):
        field_of(k)
        last = k == count - 1
        for c in range(chunks):
            potential_rows(k, c)
            send_rows(k, c, range(half, apart) if last else far, far_copies)
            send_rows(k, c, near, near_copies)
            keep_rows(k, c)
            if c == 0 and not last:
                bias_of(k + 1)
        if last:
            late_copy.start()

    for k in range(final):
        for degree in range(1, 5):
            def product_rows(base):
                at = pl.ds(pl.multiple_of(base, strip), strip)
                before = walkers_ref[k] if degree == 1 else term[degree % 2]
                product = (-STEP_ROOT / degree) * jnp.dot(
                    v_recv[k, at, :], before, preferred_element_type=jnp.float32
                )
                so_far = walkers_ref[k, at, :].astype(jnp.float32) if degree == 1 else running[at, :]
                if degree == 4:
                    out_ref[k, at, :] = (so_far + product).astype(jnp.bfloat16)
                else:
                    running[at, :] = so_far + product
                    term[(degree + 1) % 2, at, :] = product.astype(jnp.bfloat16)

            if degree == 1:
                for copy in near_copies[k]:
                    copy.wait_recv()
                product_rows(side * strip)
                for copy in far_copies[k]:
                    copy.wait_recv()
                product_rows((1 - side) * strip)
            else:
                product_rows(0)
                product_rows(strip)

    for copy in (*near_copies[final], *far_copies[final]):
        copy.wait_recv()
    scale = [-STEP_ROOT / degree for degree in range(1, 5)]
    halves = [slice(0, strip), slice(strip, 2 * strip)]
    for degree in range(1, 5):
        before = walkers_ref[final] if degree == 1 else series[degree - 2]
        for at in halves:
            product = scale[degree - 1] * jnp.dot(v_recv[final, at, :], before, preferred_element_type=jnp.float32)
            so_far = walkers_ref[final, at, :].astype(jnp.float32) if degree == 1 else running[at, :]
            running[at, :] = so_far + product
            if degree < 4:
                series[degree - 1, at, :] = product.astype(jnp.bfloat16)
    tied[:, :rows] = v_recv[final, :, late_at]
    for power in range(1, 3):
        before = tied[:, (power - 1) * rows : power * rows]
        for at in halves:
            tied[at, power * rows : (power + 1) * rows] = jnp.dot(
                v_recv[final, at, :], before, preferred_element_type=jnp.float32
            ).astype(jnp.bfloat16)

    def times(left, right):
        return jnp.dot(left, right, preferred_element_type=jnp.float32)

    late_copy.wait_recv()
    late_rows = late[...]
    own = late[:, late_at]
    first = scale[0] * times(late_rows, walkers_ref[final])
    term_1 = first.astype(jnp.bfloat16)
    second = scale[1] * (times(late_rows, series[0]) + times(own, term_1))
    term_2 = second.astype(jnp.bfloat16)
    back = times(late_rows, tied[:, : 2 * rows]).astype(jnp.bfloat16)
    third = scale[2] * (
        times(late_rows, series[1]) + scale[1] * times(back[:, :rows], term_1) + times(own, term_2)
    )
    term_3 = third.astype(jnp.bfloat16)
    fourth = scale[3] * (
        times(late_rows, series[2])
        + scale[2] * (scale[1] * times(back[:, rows:], term_1) + times(back[:, :rows], term_2))
        + times(own, term_3)
    )
    late_sum[:rows] = (scale[1] * first + scale[2] * second + scale[3] * third).astype(jnp.bfloat16)
    late_sum[rows : 2 * rows] = (scale[2] * (scale[1] * first + scale[3] * second)).astype(jnp.bfloat16)
    late_sum[2 * rows :] = (scale[3] * scale[2] * scale[1] * first).astype(jnp.bfloat16)
    for at in halves:
        out_ref[final, at, :] = (running[at, :] + times(tied[at, :], late_sum[...])).astype(jnp.bfloat16)
    out_ref[final, late_at, :] = (running[late_at, :] + first + second + third + fourth).astype(jnp.bfloat16)

    for group in (*green_copies, part_copies, [half_copies], near_copies, far_copies, [[late_copy]]):
        for copies in group:
            for copy in copies:
                copy.wait_send()


def per_device(walkers, intersection_inverse, noise_index, cholesky):
    count, orbitals, electrons = walkers.shape
    vectors, rows = cholesky.shape[:2]
    along_wa = lax.axis_size("wa")
    along_col = lax.axis_size("col")
    planes = along_wa * along_col
    if rows % LANES or planes != SUBLANES or vectors > SPLIT:
        return exchange_form(walkers, intersection_inverse, noise_index, cholesky)
    blocks = rows // BLOCK
    chunks = 1
    pieces = 2
    deep, wide = vectors * BLOCK, planes * BLOCK
    vmem = pl.BlockSpec(memory_space=pltpu.VMEM)
    sem = pltpu.SemaphoreType.DMA
    walkers_new, log_weight = pl.pallas_call(
        functools.partial(step_kernel, along_wa, along_col, chunks, pieces),
        out_shape=(
            jax.ShapeDtypeStruct(walkers.shape, jnp.bfloat16),
            jax.ShapeDtypeStruct((count,), jnp.float32),
        ),
        in_specs=[pl.BlockSpec(memory_space=pltpu.HBM)] * 4,
        out_specs=(vmem, pl.BlockSpec(memory_space=pltpu.SMEM)),
        scratch_shapes=[
            pltpu.VMEM(walkers.shape, jnp.bfloat16),
            pltpu.VMEM(intersection_inverse.shape, jnp.bfloat16),
            pltpu.VMEM(noise_index.shape, jnp.int32),
            pltpu.VMEM((blocks, vectors, BLOCK, orbitals), jnp.bfloat16),
            pltpu.VMEM((count, orbitals, electrons), jnp.bfloat16),
            pltpu.VMEM((count, planes, rows, electrons), jnp.bfloat16),
            pltpu.VMEM((count, planes, LANES), jnp.float32),
            pltpu.VMEM((count, planes, planes, LANES), jnp.float32),
            pltpu.VMEM((count, planes, LANES), jnp.float32),
            pltpu.VMEM((count, planes, LANES), jnp.float32),
            pltpu.VMEM((count, planes, rows, orbitals), jnp.bfloat16),
            pltpu.VMEM((count, orbitals, orbitals), jnp.bfloat16),
            pltpu.VMEM((deep, wide), jnp.float32),
            pltpu.VMEM((wide, deep), jnp.bfloat16),
            pltpu.VMEM((2, orbitals, electrons), jnp.bfloat16),
            pltpu.VMEM((orbitals, electrons), jnp.float32),
            pltpu.VMEM((rows, orbitals), jnp.bfloat16),
            pltpu.VMEM((3, orbitals, electrons), jnp.bfloat16),
            pltpu.VMEM((orbitals, 3 * rows), jnp.bfloat16),
            pltpu.VMEM((3 * rows, electrons), jnp.bfloat16),
            sem((3, count)), sem((blocks,)),
            sem((count, planes, pieces)), sem((count, planes, pieces)),
            sem((count, planes)), sem((count, planes)), sem((count,)), sem((count,)),
            sem((count, chunks, planes)), sem((count, chunks, planes)),
        ],
        compiler_params=pltpu.CompilerParams(
            collective_id=0, has_side_effects=True, vmem_limit_bytes=52736 * 1024
        ),
    )(walkers, intersection_inverse, noise_index, cholesky)
    return walkers_new, log_weight


def solution(mesh):
    placed = (
        P(("grp", "wa", "col", "row"), None, None),
        P(("grp", "wa", "col", "row"), None, None),
        P(("grp", "wa", "col", "row"), None),
        P(None, ("wa", "col"), None),
    )
    return jax.shard_map(
        per_device,
        mesh=mesh,
        in_specs=placed,
        out_specs=(P(("grp", "wa", "col", "row"), None, None), P(("grp", "wa", "col", "row"))),
        check_vma=False,
    )
```

```python
import functools

import jax
import jax.numpy as jnp
from jax import lax
from jax.experimental import pallas as pl
from jax.experimental.pallas import tpu as pltpu
from jax.sharding import PartitionSpec as P

NOISE_LEVELS = 65536


STEP_ROOT = 0.1
BIAS_CAP = 1.0
ROOT_TWO = 1.4142135623730951


def force_terms(green_tiles, half_tile):
    return jnp.einsum("ksf,gf->ksg", green_tiles, half_tile, preferred_element_type=jnp.float32)


def shift_field(bias_sum, code_block):
    force_bias = jnp.clip(STEP_ROOT * bias_sum, -BIAS_CAP, BIAS_CAP)
    level = (code_block.astype(jnp.float32) + 0.5) / NOISE_LEVELS
    noise = ROOT_TWO * lax.erf_inv(2.0 * level - 1.0)
    shifted = noise - force_bias
    log_step = jnp.sum(shifted * force_bias - 0.5 * force_bias * force_bias, axis=-1)
    return (shifted.astype(jnp.bfloat16), log_step)


def exchange_form(walkers, intersection_inverse, noise_index, cholesky):
    walker_count = walkers.shape[0]
    orbitals = walkers.shape[1]
    electrons = walkers.shape[2]
    vectors = cholesky.shape[0]
    tile_rows = cholesky.shape[1]
    along_wa = lax.axis_size("wa")
    along_col = lax.axis_size("col")
    planes = along_wa * along_col
    green_half = jnp.einsum(
        "kpe,kef->kpf", walkers, intersection_inverse, preferred_element_type=jnp.float32
    ).astype(jnp.bfloat16)
    packed = green_half.reshape(walker_count, planes, tile_rows * electrons)
    half_tile = cholesky[:, :, :electrons].reshape(vectors, tile_rows * electrons)
    partial_sums = force_terms(
        lax.all_to_all(packed, ("wa", "col"), split_axis=1, concat_axis=1, tiled=True), half_tile
    )
    bias_sum = lax.psum(partial_sums, ("wa", "col"))
    gathered = lax.all_gather(noise_index, ("wa", "col"), axis=0, tiled=True)
    gathered = jnp.transpose(gathered.reshape(planes, walker_count, vectors), (1, 0, 2))
    field, log_all = shift_field(bias_sum, gathered)
    log_weight = lax.dynamic_slice_in_dim(log_all, lax.axis_index(("wa", "col")), 1, 1)[:, 0]
    full_tile = cholesky.reshape(vectors, tile_rows * orbitals)
    tiles_out = jnp.einsum(
        "ksg,gf->ksf", field, full_tile, preferred_element_type=jnp.float32
    ).astype(jnp.bfloat16)
    returned = lax.all_to_all(tiles_out, ("wa", "col"), split_axis=1, concat_axis=1, tiled=True)
    potential = returned.reshape(walker_count, orbitals, orbitals)
    running = walkers.astype(jnp.float32)
    factor_term = walkers
    for degree in range(1, 5):
        product = (
            -STEP_ROOT
            / degree
            * jnp.einsum("kpq,kqe->kpe", potential, factor_term, preferred_element_type=jnp.float32)
        )
        running = running + product
        factor_term = product.astype(jnp.bfloat16)
    return (running.astype(jnp.bfloat16), log_weight)


BLOCK = 16
LANES = 128
SPLIT = LANES // 2
SUBLANES = 8
MESH = pl.DeviceIdType.MESH


def step_kernel(
    along_wa, along_col, chunks, pieces,
    walkers_hbm, inverse_hbm, noise_hbm, chol_hbm, out_ref, log_ref,
    walkers_ref, inverse_ref, noise_ref,
    chol, green_send, green_recv, part_send, part_recv, half_send, half_recv, v_send, v_recv, total, spread, term, running,
    late, series, tied, late_sum, in_sem, chol_sem, gs, gr, ps, pr, hs, hr, vs, vr,
):
    planes = along_wa * along_col
    count, orbitals, electrons = walkers_ref.shape
    blocks, vectors = chol.shape[0], chol.shape[1]
    rows = blocks * BLOCK
    wide = planes * BLOCK
    deep = vectors * BLOCK
    me = lax.axis_index("wa") * along_col + lax.axis_index("col")
    half = planes // 2
    hops = range(1, planes)
    near, far = range(1, half), range(half, planes)

    def peer(d):
        b = me
        for bit in (1 << i for i in range(planes.bit_length() - 1)):
            if d & bit:
                b = b + bit * (1 - 2 * lax.rem(me // bit, 2))
        return b, {"wa": b // along_col, "col": lax.rem(b, along_col)}

    loads = [
        pltpu.make_async_copy(chol_hbm.at[:, pl.ds(b * BLOCK, BLOCK), :], chol.at[b], chol_sem.at[b])
        for b in range(blocks)
    ]
    barrier = pltpu.get_barrier_semaphore()
    for d in reversed(hops):
        pl.semaphore_signal(barrier, inc=1, device_id=peer(d)[1], device_id_type=MESH)
    inputs = [
        pltpu.make_async_copy(hbm.at[k], ref.at[k], in_sem.at[i, k])
        for k in range(count)
        for i, (hbm, ref) in enumerate(((walkers_hbm, walkers_ref), (inverse_hbm, inverse_ref)))
    ]
    inputs.append(pltpu.make_async_copy(noise_hbm, noise_ref, in_sem.at[2, 0]))
    for load in inputs:
        load.start()

    strip = half * rows

    side = me // half

    def green_of(k, base):
        at = pl.ds(pl.multiple_of(base, strip), strip)
        green_send[k, at, :] = jnp.dot(
            walkers_ref[k, at, :], inverse_ref[k], preferred_element_type=jnp.float32
        ).astype(jnp.bfloat16)

    piece_rows = rows // pieces

    def send_green(k, those):
        for j, d in those:
            b, device = peer(d)
            copy = pltpu.make_async_remote_copy(
                src_ref=green_send.at[k, pl.ds(pl.multiple_of(b * rows + j * piece_rows, BLOCK), piece_rows), :],
                dst_ref=green_recv.at[k, me, pl.ds(j * piece_rows, piece_rows), :],
                send_sem=gs.at[k, d, j],
                recv_sem=gr.at[k, d, j],
                device_id=device,
                device_id_type=MESH,
            )
            copy.start()
            green_copies[k][j].append(copy)

    def keep_green(k):
        green_recv[k, me] = green_send[k, pl.ds(pl.multiple_of(me * rows, rows), rows), :]

    green_copies = [[[] for j in range(pieces)] for k in range(count)]
    across = [(j, d) for j in range(pieces) for d in (*far[::2], *far[1::2])]
    beside = [(j, d) for j in range(pieces) for d in near]
    held = len(across) // 2 + 1
    for k in range(count):
        for load in inputs[2 * k : 2 * k + 2]:
            load.wait()
        green_of(k, (1 - side) * strip)
        if k == 0:
            pl.semaphore_wait(barrier, planes - 1)
        if k < 2:
            send_green(k, across if k == 0 else across[:held])
        if k == 0:
            for load in loads:
                load.start()
        green_of(k, side * strip)
        if k < 2:
            send_green(k, beside)
        keep_green(k)
    for load in (inputs[-1], *loads):
        load.wait()

    row_in = lax.broadcasted_iota(jnp.int32, (deep, wide), 0) % BLOCK
    col_in = lax.broadcasted_iota(jnp.int32, (deep, wide), 1) % BLOCK
    pick = (
        lax.broadcasted_iota(jnp.int32, (planes, wide), 1) // BLOCK
        == lax.broadcasted_iota(jnp.int32, (planes, wide), 0)
    ).astype(jnp.float32)

    def noise_of(k):
        level = (noise_ref[k : k + 1, :].astype(jnp.float32) + 0.5) / NOISE_LEVELS
        return ROOT_TWO * lax.erf_inv(2.0 * level - 1.0)

    def partial_of(k):
        each_piece = blocks // pieces

        def block_dot(i):
            left = chol[i, :, :, :electrons].reshape(deep, electrons)
            right = green_recv[k, :, i * BLOCK : (i + 1) * BLOCK, :].reshape(wide, electrons)
            return lax.dot_general(left, right, (((1,), (1,)), ((), ())), preferred_element_type=jnp.float32)

        for j in range(pieces):
            for copy in green_copies[k][j]:
                copy.wait_recv()
            summed = block_dot(j * each_piece)
            for i in range(j * each_piece + 1, (j + 1) * each_piece):
                summed = summed + block_dot(i)
            total[...] = summed if j == 0 else total[...] + summed
        kept = jnp.where(row_in == col_in, total[...], 0.0).reshape(vectors, BLOCK, wide).sum(axis=1)
        sums = lax.dot_general(
            pick, kept, (((1,), (1,)), ((), ())),
            preferred_element_type=jnp.float32, precision=lax.Precision.HIGHEST,
        )
        own = lax.broadcasted_iota(jnp.int32, (planes, vectors), 0) == me
        part_send[k, :, :vectors] = sums
        part_send[k, :, SPLIT : SPLIT + vectors] = jnp.where(own, noise_of(k), 0.0)

    def send_part(k):
        copies = []
        for d in near:
            copy = pltpu.make_async_remote_copy(
                src_ref=part_send.at[k],
                dst_ref=part_recv.at[k, me],
                send_sem=ps.at[k, d],
                recv_sem=pr.at[k, d],
                device_id=peer(d)[1],
                device_id_type=MESH,
            )
            copy.start()
            copies.append(copy)
        part_recv[k, me] = part_send[k]
        return copies

    half_copies = [
        pltpu.make_async_remote_copy(
            src_ref=half_send.at[k],
            dst_ref=half_recv.at[k],
            send_sem=hs.at[k],
            recv_sem=hr.at[k],
            device_id=peer(half)[1],
            device_id_type=MESH,
        )
        for k in range(count)
    ]

    def send_half(k):
        for copy in part_copies[k]:
            copy.wait_recv()
        summed = part_recv[k, side * half]
        for a in range(1, half):
            summed = summed + part_recv[k, side * half + a]
        half_send[k] = summed
        half_copies[k].start()

    plane_row = lax.broadcasted_iota(jnp.int32, (planes, LANES), 0)
    vector_lane = lax.broadcasted_iota(jnp.int32, (planes, LANES), 1) < SPLIT

    def spread_field(k):
        both = half_send[k] + half_recv[k]
        bias_sum = jnp.where(vector_lane, both, 0.0)
        noise = jnp.where(vector_lane, pltpu.roll(both, LANES - SPLIT, 1), 0.0)
        force = jnp.clip(STEP_ROOT * bias_sum, -BIAS_CAP, BIAS_CAP)
        shifted = noise - force
        steps = jnp.where(plane_row == me, shifted * force - 0.5 * force * force, 0.0)
        log_ref[k] = jnp.sum(steps)
        field = shifted.astype(jnp.bfloat16)
        tall = (
            lax.broadcasted_iota(jnp.int32, (wide, planes), 0) // BLOCK
            == lax.broadcasted_iota(jnp.int32, (wide, planes), 1)
        ).astype(jnp.float32)
        by_row = jnp.dot(tall, field.astype(jnp.float32), preferred_element_type=jnp.float32)
        out = (
            lax.broadcasted_iota(jnp.int32, (LANES, deep), 1) // BLOCK
            == lax.broadcasted_iota(jnp.int32, (LANES, deep), 0)
        ).astype(jnp.float32).astype(jnp.bfloat16)
        both = jnp.dot(by_row.astype(jnp.bfloat16), out, preferred_element_type=jnp.float32)
        same = (
            lax.broadcasted_iota(jnp.int32, (wide, deep), 0) % BLOCK
            == lax.broadcasted_iota(jnp.int32, (wide, deep), 1) % BLOCK
        )
        spread[...] = jnp.where(same, both, 0.0).astype(jnp.bfloat16)

    each = blocks // chunks
    part_rows = each * BLOCK

    def potential_rows(k, c):
        def body(i, carry):
            b = c * each + i
            tile = jnp.dot(
                spread[...], chol[b].reshape(deep, orbitals), preferred_element_type=jnp.float32
            ).astype(jnp.bfloat16)
            v_send[k, :, pl.ds(pl.multiple_of(b * BLOCK, BLOCK), BLOCK), :] = tile.reshape(
                planes, BLOCK, orbitals
            )
            return carry

        lax.fori_loop(0, each, body, 0)

    def mine(c):
        return pl.ds(pl.multiple_of(me * rows + c * part_rows, BLOCK), part_rows)

    final = count - 1
    apart = planes - 1
    late_at = pl.ds(pl.multiple_of(peer(apart)[0] * rows, rows), rows)
    v_recv[final, late_at, :] = jnp.zeros((rows, orbitals), jnp.bfloat16)
    late_copy = pltpu.make_async_remote_copy(
        src_ref=v_send.at[final, peer(apart)[0]],
        dst_ref=late,
        send_sem=vs.at[final, 0, apart],
        recv_sem=vr.at[final, 0, apart],
        device_id=peer(apart)[1],
        device_id_type=MESH,
    )
    near_copies = [[] for k in range(count)]
    far_copies = [[] for k in range(count)]

    def send_rows(k, c, those, kept):
        for d in those:
            b, device = peer(d)
            copy = pltpu.make_async_remote_copy(
                src_ref=v_send.at[k, b, pl.ds(c * part_rows, part_rows), :],
                dst_ref=v_recv.at[k, mine(c), :],
                send_sem=vs.at[k, c, d],
                recv_sem=vr.at[k, c, d],
                device_id=device,
                device_id_type=MESH,
            )
            copy.start()
            kept[k].append(copy)

    def keep_rows(k, c):
        v_recv[k, mine(c), :] = v_send[k, me, pl.ds(c * part_rows, part_rows), :]

    part_send[...] = jnp.zeros_like(part_send)
    part_copies = []

    def bias_of(k):
        partial_of(k)
        part_copies.append(send_part(k))
        send_half(k)

    def field_of(k):
        half_copies[k].wait_recv()
        spread_field(k)

    bias_of(0)
    if count > 1:
        send_green(1, across[held:])
    for k in range(2, count):
        send_green(k, across + beside)
    for k in range(count):
        field_of(k)
        last = k == count - 1
        for c in range(chunks):
            potential_rows(k, c)
            send_rows(k, c, range(half, apart) if last else far, far_copies)
            send_rows(k, c, near, near_copies)
            keep_rows(k, c)
            if c == 0 and not last:
                bias_of(k + 1)
        if last:
            late_copy.start()

    for k in range(final):
        for degree in range(1, 5):
            def product_rows(base):
                at = pl.ds(pl.multiple_of(base, strip), strip)
                before = walkers_ref[k] if degree == 1 else term[degree % 2]
                product = (-STEP_ROOT / degree) * jnp.dot(
                    v_recv[k, at, :], before, preferred_element_type=jnp.float32
                )
                so_far = walkers_ref[k, at, :].astype(jnp.float32) if degree == 1 else running[at, :]
                if degree == 4:
                    out_ref[k, at, :] = (so_far + product).astype(jnp.bfloat16)
                else:
                    running[at, :] = so_far + product
                    term[(degree + 1) % 2, at, :] = product.astype(jnp.bfloat16)

            if degree == 1:
                for copy in near_copies[k]:
                    copy.wait_recv()
                product_rows(side * strip)
                for copy in far_copies[k]:
                    copy.wait_recv()
                product_rows((1 - side) * strip)
            else:
                product_rows(0)
                product_rows(strip)

    for copy in (*near_copies[final], *far_copies[final]):
        copy.wait_recv()
    scale = [-STEP_ROOT / degree for degree in range(1, 5)]
    halves = [slice(0, strip), slice(strip, 2 * strip)]
    for degree in range(1, 5):
        before = walkers_ref[final] if degree == 1 else series[degree - 2]
        for at in halves:
            product = scale[degree - 1] * jnp.dot(v_recv[final, at, :], before, preferred_element_type=jnp.float32)
            so_far = walkers_ref[final, at, :].astype(jnp.float32) if degree == 1 else running[at, :]
            running[at, :] = so_far + product
            if degree < 4:
                series[degree - 1, at, :] = product.astype(jnp.bfloat16)
    tied[:, :rows] = v_recv[final, :, late_at]
    for power in range(1, 3):
        before = tied[:, (power - 1) * rows : power * rows]
        for at in halves:
            tied[at, power * rows : (power + 1) * rows] = jnp.dot(
                v_recv[final, at, :], before, preferred_element_type=jnp.float32
            ).astype(jnp.bfloat16)

    def times(left, right):
        return jnp.dot(left, right, preferred_element_type=jnp.float32)

    late_copy.wait_recv()
    late_rows = late[...]
    own = late[:, late_at]
    first = scale[0] * times(late_rows, walkers_ref[final])
    term_1 = first.astype(jnp.bfloat16)
    second = scale[1] * (times(late_rows, series[0]) + times(own, term_1))
    term_2 = second.astype(jnp.bfloat16)
    back = times(late_rows, tied[:, : 2 * rows]).astype(jnp.bfloat16)
    third = scale[2] * (
        times(late_rows, series[1]) + scale[1] * times(back[:, :rows], term_1) + times(own, term_2)
    )
    term_3 = third.astype(jnp.bfloat16)
    fourth = scale[3] * (
        times(late_rows, series[2])
        + scale[2] * (scale[1] * times(back[:, rows:], term_1) + times(back[:, :rows], term_2))
        + times(own, term_3)
    )
    late_sum[:rows] = (scale[1] * first + scale[2] * second + scale[3] * third).astype(jnp.bfloat16)
    late_sum[rows : 2 * rows] = (scale[2] * (scale[1] * first + scale[3] * second)).astype(jnp.bfloat16)
    late_sum[2 * rows :] = (scale[3] * scale[2] * scale[1] * first).astype(jnp.bfloat16)
    for at in halves:
        out_ref[final, at, :] = (running[at, :] + times(tied[at, :], late_sum[...])).astype(jnp.bfloat16)
    out_ref[final, late_at, :] = (running[late_at, :] + first + second + third + fourth).astype(jnp.bfloat16)

    for group in (*green_copies, part_copies, [half_copies], near_copies, far_copies, [[late_copy]]):
        for copies in group:
            for copy in copies:
                copy.wait_send()


def per_device(walkers, intersection_inverse, noise_index, cholesky):
    count, orbitals, electrons = walkers.shape
    vectors, rows = cholesky.shape[:2]
    along_wa = lax.axis_size("wa")
    along_col = lax.axis_size("col")
    planes = along_wa * along_col
    if rows % LANES or planes != SUBLANES or vectors > SPLIT:
        return exchange_form(walkers, intersection_inverse, noise_index, cholesky)
    blocks = rows // BLOCK
    chunks = 1
    pieces = 2
    deep, wide = vectors * BLOCK, planes * BLOCK
    vmem = pl.BlockSpec(memory_space=pltpu.VMEM)
    sem = pltpu.SemaphoreType.DMA
    walkers_new, log_weight = pl.pallas_call(
        functools.partial(step_kernel, along_wa, along_col, chunks, pieces),
        out_shape=(
            jax.ShapeDtypeStruct(walkers.shape, jnp.bfloat16),
            jax.ShapeDtypeStruct((count,), jnp.float32),
        ),
        in_specs=[pl.BlockSpec(memory_space=pltpu.HBM)] * 4,
        out_specs=(vmem, pl.BlockSpec(memory_space=pltpu.SMEM)),
        scratch_shapes=[
            pltpu.VMEM(walkers.shape, jnp.bfloat16),
            pltpu.VMEM(intersection_inverse.shape, jnp.bfloat16),
            pltpu.VMEM(noise_index.shape, jnp.int32),
            pltpu.VMEM((blocks, vectors, BLOCK, orbitals), jnp.bfloat16),
            pltpu.VMEM((count, orbitals, electrons), jnp.bfloat16),
            pltpu.VMEM((count, planes, rows, electrons), jnp.bfloat16),
            pltpu.VMEM((count, planes, LANES), jnp.float32),
            pltpu.VMEM((count, planes, planes, LANES), jnp.float32),
            pltpu.VMEM((count, planes, LANES), jnp.float32),
            pltpu.VMEM((count, planes, LANES), jnp.float32),
            pltpu.VMEM((count, planes, rows, orbitals), jnp.bfloat16),
            pltpu.VMEM((count, orbitals, orbitals), jnp.bfloat16),
            pltpu.VMEM((deep, wide), jnp.float32),
            pltpu.VMEM((wide, deep), jnp.bfloat16),
            pltpu.VMEM((2, orbitals, electrons), jnp.bfloat16),
            pltpu.VMEM((orbitals, electrons), jnp.float32),
            pltpu.VMEM((rows, orbitals), jnp.bfloat16),
            pltpu.VMEM((3, orbitals, electrons), jnp.bfloat16),
            pltpu.VMEM((orbitals, 3 * rows), jnp.bfloat16),
            pltpu.VMEM((3 * rows, electrons), jnp.bfloat16),
            sem((3, count)), sem((blocks,)),
            sem((count, planes, pieces)), sem((count, planes, pieces)),
            sem((count, planes)), sem((count, planes)), sem((count,)), sem((count,)),
            sem((count, chunks, planes)), sem((count, chunks, planes)),
        ],
        compiler_params=pltpu.CompilerParams(
            collective_id=0, has_side_effects=True, vmem_limit_bytes=52736 * 1024
        ),
    )(walkers, intersection_inverse, noise_index, cholesky)
    return walkers_new, log_weight


def solution(mesh):
    placed = (
        P(("grp", "wa", "col", "row"), None, None),
        P(("grp", "wa", "col", "row"), None, None),
        P(("grp", "wa", "col", "row"), None),
        P(None, ("wa", "col"), None),
    )
    return jax.shard_map(
        per_device,
        mesh=mesh,
        in_specs=placed,
        out_specs=(P(("grp", "wa", "col", "row"), None, None), P(("grp", "wa", "col", "row"))),
        check_vma=False,
    )
```

```python
import functools

import jax
import jax.numpy as jnp
from jax import lax
from jax.experimental import pallas as pl
from jax.experimental.pallas import tpu as pltpu
from jax.sharding import PartitionSpec as P

NOISE_LEVELS = 65536


STEP_ROOT = 0.1
BIAS_CAP = 1.0
ROOT_TWO = 1.4142135623730951


def force_terms(green_tiles, half_tile):
    return jnp.einsum("ksf,gf->ksg", green_tiles, half_tile, preferred_element_type=jnp.float32)


def shift_field(bias_sum, code_block):
    force_bias = jnp.clip(STEP_ROOT * bias_sum, -BIAS_CAP, BIAS_CAP)
    level = (code_block.astype(jnp.float32) + 0.5) / NOISE_LEVELS
    noise = ROOT_TWO * lax.erf_inv(2.0 * level - 1.0)
    shifted = noise - force_bias
    log_step = jnp.sum(shifted * force_bias - 0.5 * force_bias * force_bias, axis=-1)
    return (shifted.astype(jnp.bfloat16), log_step)


def exchange_form(walkers, intersection_inverse, noise_index, cholesky):
    walker_count = walkers.shape[0]
    orbitals = walkers.shape[1]
    electrons = walkers.shape[2]
    vectors = cholesky.shape[0]
    tile_rows = cholesky.shape[1]
    along_wa = lax.axis_size("wa")
    along_col = lax.axis_size("col")
    planes = along_wa * along_col
    green_half = jnp.einsum(
        "kpe,kef->kpf", walkers, intersection_inverse, preferred_element_type=jnp.float32
    ).astype(jnp.bfloat16)
    packed = green_half.reshape(walker_count, planes, tile_rows * electrons)
    half_tile = cholesky[:, :, :electrons].reshape(vectors, tile_rows * electrons)
    partial_sums = force_terms(
        lax.all_to_all(packed, ("wa", "col"), split_axis=1, concat_axis=1, tiled=True), half_tile
    )
    bias_sum = lax.psum(partial_sums, ("wa", "col"))
    gathered = lax.all_gather(noise_index, ("wa", "col"), axis=0, tiled=True)
    gathered = jnp.transpose(gathered.reshape(planes, walker_count, vectors), (1, 0, 2))
    field, log_all = shift_field(bias_sum, gathered)
    log_weight = lax.dynamic_slice_in_dim(log_all, lax.axis_index(("wa", "col")), 1, 1)[:, 0]
    full_tile = cholesky.reshape(vectors, tile_rows * orbitals)
    tiles_out = jnp.einsum(
        "ksg,gf->ksf", field, full_tile, preferred_element_type=jnp.float32
    ).astype(jnp.bfloat16)
    returned = lax.all_to_all(tiles_out, ("wa", "col"), split_axis=1, concat_axis=1, tiled=True)
    potential = returned.reshape(walker_count, orbitals, orbitals)
    running = walkers.astype(jnp.float32)
    factor_term = walkers
    for degree in range(1, 5):
        product = (
            -STEP_ROOT
            / degree
            * jnp.einsum("kpq,kqe->kpe", potential, factor_term, preferred_element_type=jnp.float32)
        )
        running = running + product
        factor_term = product.astype(jnp.bfloat16)
    return (running.astype(jnp.bfloat16), log_weight)


BLOCK = 16
LANES = 128
SPLIT = LANES // 2
SUBLANES = 8
MESH = pl.DeviceIdType.MESH


def step_kernel(
    along_wa, along_col, chunks, pieces,
    walkers_hbm, inverse_hbm, noise_hbm, chol_hbm, out_ref, log_ref,
    walkers_ref, inverse_ref, noise_ref,
    chol, green_send, green_recv, part_send, part_recv, half_send, half_recv, v_send, v_recv, total, spread, term, running,
    late, series, tied, late_sum, in_sem, chol_sem, gs, gr, ps, pr, hs, hr, vs, vr,
):
    planes = along_wa * along_col
    count, orbitals, electrons = walkers_ref.shape
    blocks, vectors = chol.shape[0], chol.shape[1]
    rows = blocks * BLOCK
    wide = planes * BLOCK
    deep = vectors * BLOCK
    me = lax.axis_index("wa") * along_col + lax.axis_index("col")
    half = planes // 2
    hops = range(1, planes)
    near, far = range(1, half), range(half, planes)

    def peer(d):
        b = me
        for bit in (1 << i for i in range(planes.bit_length() - 1)):
            if d & bit:
                b = b + bit * (1 - 2 * lax.rem(me // bit, 2))
        return b, {"wa": b // along_col, "col": lax.rem(b, along_col)}

    loads = [
        pltpu.make_async_copy(chol_hbm.at[:, pl.ds(b * BLOCK, BLOCK), :], chol.at[b], chol_sem.at[b])
        for b in range(blocks)
    ]
    barrier = pltpu.get_barrier_semaphore()
    for d in reversed(hops):
        pl.semaphore_signal(barrier, inc=1, device_id=peer(d)[1], device_id_type=MESH)
    inputs = [
        pltpu.make_async_copy(hbm.at[k], ref.at[k], in_sem.at[i, k])
        for k in range(count)
        for i, (hbm, ref) in enumerate(((walkers_hbm, walkers_ref), (inverse_hbm, inverse_ref)))
    ]
    inputs.append(pltpu.make_async_copy(noise_hbm, noise_ref, in_sem.at[2, 0]))
    for load in inputs:
        load.start()

    strip = half * rows

    side = me // half

    def green_of(k, base):
        at = pl.ds(pl.multiple_of(base, strip), strip)
        green_send[k, at, :] = jnp.dot(
            walkers_ref[k, at, :], inverse_ref[k], preferred_element_type=jnp.float32
        ).astype(jnp.bfloat16)

    piece_rows = rows // pieces

    def send_green(k, those):
        for j, d in those:
            b, device = peer(d)
            copy = pltpu.make_async_remote_copy(
                src_ref=green_send.at[k, pl.ds(pl.multiple_of(b * rows + j * piece_rows, BLOCK), piece_rows), :],
                dst_ref=green_recv.at[k, me, pl.ds(j * piece_rows, piece_rows), :],
                send_sem=gs.at[k, d, j],
                recv_sem=gr.at[k, d, j],
                device_id=device,
                device_id_type=MESH,
            )
            copy.start()
            green_copies[k][j].append(copy)

    def keep_green(k):
        green_recv[k, me] = green_send[k, pl.ds(pl.multiple_of(me * rows, rows), rows), :]

    green_copies = [[[] for j in range(pieces)] for k in range(count)]
    across = [(j, d) for j in range(pieces) for d in (*far[::2], *far[1::2])]
    beside = [(j, d) for j in range(pieces) for d in near]
    held = len(across) // 2 + 1
    for k in range(count):
        for load in inputs[2 * k : 2 * k + 2]:
            load.wait()
        green_of(k, (1 - side) * strip)
        if k == 0:
            pl.semaphore_wait(barrier, planes - 1)
        if k < 2:
            send_green(k, across if k == 0 else across[:held])
        green_of(k, side * strip)
        if k < 2:
            send_green(k, beside)
        keep_green(k)
    for load in loads:
        load.start()
    for load in (inputs[-1], *loads):
        load.wait()

    row_in = lax.broadcasted_iota(jnp.int32, (deep, wide), 0) % BLOCK
    col_in = lax.broadcasted_iota(jnp.int32, (deep, wide), 1) % BLOCK
    pick = (
        lax.broadcasted_iota(jnp.int32, (planes, wide), 1) // BLOCK
        == lax.broadcasted_iota(jnp.int32, (planes, wide), 0)
    ).astype(jnp.float32)

    def noise_of(k):
        level = (noise_ref[k : k + 1, :].astype(jnp.float32) + 0.5) / NOISE_LEVELS
        return ROOT_TWO * lax.erf_inv(2.0 * level - 1.0)

    def partial_of(k):
        each_piece = blocks // pieces

        def block_dot(i):
            left = chol[i, :, :, :electrons].reshape(deep, electrons)
            right = green_recv[k, :, i * BLOCK : (i + 1) * BLOCK, :].reshape(wide, electrons)
            return lax.dot_general(left, right, (((1,), (1,)), ((), ())), preferred_element_type=jnp.float32)

        for j in range(pieces):
            for copy in green_copies[k][j]:
                copy.wait_recv()
            summed = block_dot(j * each_piece)
            for i in range(j * each_piece + 1, (j + 1) * each_piece):
                summed = summed + block_dot(i)
            total[...] = summed if j == 0 else total[...] + summed
        kept = jnp.where(row_in == col_in, total[...], 0.0).reshape(vectors, BLOCK, wide).sum(axis=1)
        sums = lax.dot_general(
            pick, kept, (((1,), (1,)), ((), ())),
            preferred_element_type=jnp.float32, precision=lax.Precision.HIGHEST,
        )
        own = lax.broadcasted_iota(jnp.int32, (planes, vectors), 0) == me
        part_send[k, :, :vectors] = sums
        part_send[k, :, SPLIT : SPLIT + vectors] = jnp.where(own, noise_of(k), 0.0)

    def send_part(k):
        copies = []
        for d in near:
            copy = pltpu.make_async_remote_copy(
                src_ref=part_send.at[k],
                dst_ref=part_recv.at[k, me],
                send_sem=ps.at[k, d],
                recv_sem=pr.at[k, d],
                device_id=peer(d)[1],
                device_id_type=MESH,
            )
            copy.start()
            copies.append(copy)
        part_recv[k, me] = part_send[k]
        return copies

    half_copies = [
        pltpu.make_async_remote_copy(
            src_ref=half_send.at[k],
            dst_ref=half_recv.at[k],
            send_sem=hs.at[k],
            recv_sem=hr.at[k],
            device_id=peer(half)[1],
            device_id_type=MESH,
        )
        for k in range(count)
    ]

    def send_half(k):
        for copy in part_copies[k]:
            copy.wait_recv()
        summed = part_recv[k, side * half]
        for a in range(1, half):
            summed = summed + part_recv[k, side * half + a]
        half_send[k] = summed
        half_copies[k].start()

    plane_row = lax.broadcasted_iota(jnp.int32, (planes, LANES), 0)
    vector_lane = lax.broadcasted_iota(jnp.int32, (planes, LANES), 1) < SPLIT

    def spread_field(k):
        both = half_send[k] + half_recv[k]
        bias_sum = jnp.where(vector_lane, both, 0.0)
        noise = jnp.where(vector_lane, pltpu.roll(both, LANES - SPLIT, 1), 0.0)
        force = jnp.clip(STEP_ROOT * bias_sum, -BIAS_CAP, BIAS_CAP)
        shifted = noise - force
        steps = jnp.where(plane_row == me, shifted * force - 0.5 * force * force, 0.0)
        log_ref[k] = jnp.sum(steps)
        field = shifted.astype(jnp.bfloat16)
        tall = (
            lax.broadcasted_iota(jnp.int32, (wide, planes), 0) // BLOCK
            == lax.broadcasted_iota(jnp.int32, (wide, planes), 1)
        ).astype(jnp.float32)
        by_row = jnp.dot(tall, field.astype(jnp.float32), preferred_element_type=jnp.float32)
        out = (
            lax.broadcasted_iota(jnp.int32, (LANES, deep), 1) // BLOCK
            == lax.broadcasted_iota(jnp.int32, (LANES, deep), 0)
        ).astype(jnp.float32).astype(jnp.bfloat16)
        both = jnp.dot(by_row.astype(jnp.bfloat16), out, preferred_element_type=jnp.float32)
        same = (
            lax.broadcasted_iota(jnp.int32, (wide, deep), 0) % BLOCK
            == lax.broadcasted_iota(jnp.int32, (wide, deep), 1) % BLOCK
        )
        spread[...] = jnp.where(same, both, 0.0).astype(jnp.bfloat16)

    each = blocks // chunks
    part_rows = each * BLOCK

    def potential_rows(k, c):
        def body(i, carry):
            b = c * each + i
            tile = jnp.dot(
                spread[...], chol[b].reshape(deep, orbitals), preferred_element_type=jnp.float32
            ).astype(jnp.bfloat16)
            v_send[k, :, pl.ds(pl.multiple_of(b * BLOCK, BLOCK), BLOCK), :] = tile.reshape(
                planes, BLOCK, orbitals
            )
            return carry

        lax.fori_loop(0, each, body, 0)

    def mine(c):
        return pl.ds(pl.multiple_of(me * rows + c * part_rows, BLOCK), part_rows)

    final = count - 1
    apart = planes - 1
    late_at = pl.ds(pl.multiple_of(peer(apart)[0] * rows, rows), rows)
    v_recv[final, late_at, :] = jnp.zeros((rows, orbitals), jnp.bfloat16)
    late_copy = pltpu.make_async_remote_copy(
        src_ref=v_send.at[final, peer(apart)[0]],
        dst_ref=late,
        send_sem=vs.at[final, 0, apart],
        recv_sem=vr.at[final, 0, apart],
        device_id=peer(apart)[1],
        device_id_type=MESH,
    )
    near_copies = [[] for k in range(count)]
    far_copies = [[] for k in range(count)]

    def send_rows(k, c, those, kept):
        for d in those:
            b, device = peer(d)
            copy = pltpu.make_async_remote_copy(
                src_ref=v_send.at[k, b, pl.ds(c * part_rows, part_rows), :],
                dst_ref=v_recv.at[k, mine(c), :],
                send_sem=vs.at[k, c, d],
                recv_sem=vr.at[k, c, d],
                device_id=device,
                device_id_type=MESH,
            )
            copy.start()
            kept[k].append(copy)

    def keep_rows(k, c):
        v_recv[k, mine(c), :] = v_send[k, me, pl.ds(c * part_rows, part_rows), :]

    part_send[...] = jnp.zeros_like(part_send)
    part_copies = []

    def bias_of(k):
        partial_of(k)
        part_copies.append(send_part(k))
        send_half(k)

    def field_of(k):
        half_copies[k].wait_recv()
        spread_field(k)

    bias_of(0)
    if count > 1:
        send_green(1, across[held:])
    for k in range(2, count):
        send_green(k, across + beside)
    for k in range(count):
        field_of(k)
        last = k == count - 1
        for c in range(chunks):
            potential_rows(k, c)
            for d, e in zip(range(half, apart), near):
                send_rows(k, c, (d,), far_copies)
                send_rows(k, c, (e,), near_copies)
            if not last:
                send_rows(k, c, (apart,), far_copies)
            keep_rows(k, c)
            if c == 0 and not last:
                bias_of(k + 1)
        if last:
            late_copy.start()

    for k in range(final):
        for degree in range(1, 5):
            def product_rows(base):
                at = pl.ds(pl.multiple_of(base, strip), strip)
                before = walkers_ref[k] if degree == 1 else term[degree % 2]
                product = (-STEP_ROOT / degree) * jnp.dot(
                    v_recv[k, at, :], before, preferred_element_type=jnp.float32
                )
                so_far = walkers_ref[k, at, :].astype(jnp.float32) if degree == 1 else running[at, :]
                if degree == 4:
                    out_ref[k, at, :] = (so_far + product).astype(jnp.bfloat16)
                else:
                    running[at, :] = so_far + product
                    term[(degree + 1) % 2, at, :] = product.astype(jnp.bfloat16)

            if degree == 1:
                for copy in near_copies[k]:
                    copy.wait_recv()
                product_rows(side * strip)
                for copy in far_copies[k]:
                    copy.wait_recv()
                product_rows((1 - side) * strip)
            else:
                product_rows(0)
                product_rows(strip)

    for copy in (*near_copies[final], *far_copies[final]):
        copy.wait_recv()
    scale = [-STEP_ROOT / degree for degree in range(1, 5)]
    halves = [slice(0, strip), slice(strip, 2 * strip)]
    for degree in range(1, 5):
        before = walkers_ref[final] if degree == 1 else series[degree - 2]
        for at in halves:
            product = scale[degree - 1] * jnp.dot(v_recv[final, at, :], before, preferred_element_type=jnp.float32)
            so_far = walkers_ref[final, at, :].astype(jnp.float32) if degree == 1 else running[at, :]
            running[at, :] = so_far + product
            if degree < 4:
                series[degree - 1, at, :] = product.astype(jnp.bfloat16)
    tied[:, :rows] = v_recv[final, :, late_at]
    for power in range(1, 3):
        before = tied[:, (power - 1) * rows : power * rows]
        for at in halves:
            tied[at, power * rows : (power + 1) * rows] = jnp.dot(
                v_recv[final, at, :], before, preferred_element_type=jnp.float32
            ).astype(jnp.bfloat16)

    def times(left, right):
        return jnp.dot(left, right, preferred_element_type=jnp.float32)

    late_copy.wait_recv()
    late_rows = late[...]
    own = late[:, late_at]
    first = scale[0] * times(late_rows, walkers_ref[final])
    term_1 = first.astype(jnp.bfloat16)
    second = scale[1] * (times(late_rows, series[0]) + times(own, term_1))
    term_2 = second.astype(jnp.bfloat16)
    back = times(late_rows, tied[:, : 2 * rows]).astype(jnp.bfloat16)
    third = scale[2] * (
        times(late_rows, series[1]) + scale[1] * times(back[:, :rows], term_1) + times(own, term_2)
    )
    term_3 = third.astype(jnp.bfloat16)
    fourth = scale[3] * (
        times(late_rows, series[2])
        + scale[2] * (scale[1] * times(back[:, rows:], term_1) + times(back[:, :rows], term_2))
        + times(own, term_3)
    )
    late_sum[:rows] = (scale[1] * first + scale[2] * second + scale[3] * third).astype(jnp.bfloat16)
    late_sum[rows : 2 * rows] = (scale[2] * (scale[1] * first + scale[3] * second)).astype(jnp.bfloat16)
    late_sum[2 * rows :] = (scale[3] * scale[2] * scale[1] * first).astype(jnp.bfloat16)
    for at in halves:
        out_ref[final, at, :] = (running[at, :] + times(tied[at, :], late_sum[...])).astype(jnp.bfloat16)
    out_ref[final, late_at, :] = (running[late_at, :] + first + second + third + fourth).astype(jnp.bfloat16)

    for group in (*green_copies, part_copies, [half_copies], near_copies, far_copies, [[late_copy]]):
        for copies in group:
            for copy in copies:
                copy.wait_send()


def per_device(walkers, intersection_inverse, noise_index, cholesky):
    count, orbitals, electrons = walkers.shape
    vectors, rows = cholesky.shape[:2]
    along_wa = lax.axis_size("wa")
    along_col = lax.axis_size("col")
    planes = along_wa * along_col
    if rows % LANES or planes != SUBLANES or vectors > SPLIT:
        return exchange_form(walkers, intersection_inverse, noise_index, cholesky)
    blocks = rows // BLOCK
    chunks = 1
    pieces = 2
    deep, wide = vectors * BLOCK, planes * BLOCK
    vmem = pl.BlockSpec(memory_space=pltpu.VMEM)
    sem = pltpu.SemaphoreType.DMA
    walkers_new, log_weight = pl.pallas_call(
        functools.partial(step_kernel, along_wa, along_col, chunks, pieces),
        out_shape=(
            jax.ShapeDtypeStruct(walkers.shape, jnp.bfloat16),
            jax.ShapeDtypeStruct((count,), jnp.float32),
        ),
        in_specs=[pl.BlockSpec(memory_space=pltpu.HBM)] * 4,
        out_specs=(vmem, pl.BlockSpec(memory_space=pltpu.SMEM)),
        scratch_shapes=[
            pltpu.VMEM(walkers.shape, jnp.bfloat16),
            pltpu.VMEM(intersection_inverse.shape, jnp.bfloat16),
            pltpu.VMEM(noise_index.shape, jnp.int32),
            pltpu.VMEM((blocks, vectors, BLOCK, orbitals), jnp.bfloat16),
            pltpu.VMEM((count, orbitals, electrons), jnp.bfloat16),
            pltpu.VMEM((count, planes, rows, electrons), jnp.bfloat16),
            pltpu.VMEM((count, planes, LANES), jnp.float32),
            pltpu.VMEM((count, planes, planes, LANES), jnp.float32),
            pltpu.VMEM((count, planes, LANES), jnp.float32),
            pltpu.VMEM((count, planes, LANES), jnp.float32),
            pltpu.VMEM((count, planes, rows, orbitals), jnp.bfloat16),
            pltpu.VMEM((count, orbitals, orbitals), jnp.bfloat16),
            pltpu.VMEM((deep, wide), jnp.float32),
            pltpu.VMEM((wide, deep), jnp.bfloat16),
            pltpu.VMEM((2, orbitals, electrons), jnp.bfloat16),
            pltpu.VMEM((orbitals, electrons), jnp.float32),
            pltpu.VMEM((rows, orbitals), jnp.bfloat16),
            pltpu.VMEM((3, orbitals, electrons), jnp.bfloat16),
            pltpu.VMEM((orbitals, 3 * rows), jnp.bfloat16),
            pltpu.VMEM((3 * rows, electrons), jnp.bfloat16),
            sem((3, count)), sem((blocks,)),
            sem((count, planes, pieces)), sem((count, planes, pieces)),
            sem((count, planes)), sem((count, planes)), sem((count,)), sem((count,)),
            sem((count, chunks, planes)), sem((count, chunks, planes)),
        ],
        compiler_params=pltpu.CompilerParams(
            collective_id=0, has_side_effects=True, vmem_limit_bytes=52736 * 1024
        ),
    )(walkers, intersection_inverse, noise_index, cholesky)
    return walkers_new, log_weight


def solution(mesh):
    placed = (
        P(("grp", "wa", "col", "row"), None, None),
        P(("grp", "wa", "col", "row"), None, None),
        P(("grp", "wa", "col", "row"), None),
        P(None, ("wa", "col"), None),
    )
    return jax.shard_map(
        per_device,
        mesh=mesh,
        in_specs=placed,
        out_specs=(P(("grp", "wa", "col", "row"), None, None), P(("grp", "wa", "col", "row"))),
        check_vma=False,
    )
```

```python
import functools

import jax
import jax.numpy as jnp
from jax import lax
from jax.experimental import pallas as pl
from jax.experimental.pallas import tpu as pltpu
from jax.sharding import PartitionSpec as P

NOISE_LEVELS = 65536


STEP_ROOT = 0.1
BIAS_CAP = 1.0
ROOT_TWO = 1.4142135623730951


def force_terms(green_tiles, half_tile):
    return jnp.einsum("ksf,gf->ksg", green_tiles, half_tile, preferred_element_type=jnp.float32)


def shift_field(bias_sum, code_block):
    force_bias = jnp.clip(STEP_ROOT * bias_sum, -BIAS_CAP, BIAS_CAP)
    level = (code_block.astype(jnp.float32) + 0.5) / NOISE_LEVELS
    noise = ROOT_TWO * lax.erf_inv(2.0 * level - 1.0)
    shifted = noise - force_bias
    log_step = jnp.sum(shifted * force_bias - 0.5 * force_bias * force_bias, axis=-1)
    return (shifted.astype(jnp.bfloat16), log_step)


def exchange_form(walkers, intersection_inverse, noise_index, cholesky):
    walker_count = walkers.shape[0]
    orbitals = walkers.shape[1]
    electrons = walkers.shape[2]
    vectors = cholesky.shape[0]
    tile_rows = cholesky.shape[1]
    along_wa = lax.axis_size("wa")
    along_col = lax.axis_size("col")
    planes = along_wa * along_col
    green_half = jnp.einsum(
        "kpe,kef->kpf", walkers, intersection_inverse, preferred_element_type=jnp.float32
    ).astype(jnp.bfloat16)
    packed = green_half.reshape(walker_count, planes, tile_rows * electrons)
    half_tile = cholesky[:, :, :electrons].reshape(vectors, tile_rows * electrons)
    partial_sums = force_terms(
        lax.all_to_all(packed, ("wa", "col"), split_axis=1, concat_axis=1, tiled=True), half_tile
    )
    bias_sum = lax.psum(partial_sums, ("wa", "col"))
    gathered = lax.all_gather(noise_index, ("wa", "col"), axis=0, tiled=True)
    gathered = jnp.transpose(gathered.reshape(planes, walker_count, vectors), (1, 0, 2))
    field, log_all = shift_field(bias_sum, gathered)
    log_weight = lax.dynamic_slice_in_dim(log_all, lax.axis_index(("wa", "col")), 1, 1)[:, 0]
    full_tile = cholesky.reshape(vectors, tile_rows * orbitals)
    tiles_out = jnp.einsum(
        "ksg,gf->ksf", field, full_tile, preferred_element_type=jnp.float32
    ).astype(jnp.bfloat16)
    returned = lax.all_to_all(tiles_out, ("wa", "col"), split_axis=1, concat_axis=1, tiled=True)
    potential = returned.reshape(walker_count, orbitals, orbitals)
    running = walkers.astype(jnp.float32)
    factor_term = walkers
    for degree in range(1, 5):
        product = (
            -STEP_ROOT
            / degree
            * jnp.einsum("kpq,kqe->kpe", potential, factor_term, preferred_element_type=jnp.float32)
        )
        running = running + product
        factor_term = product.astype(jnp.bfloat16)
    return (running.astype(jnp.bfloat16), log_weight)


BLOCK = 16
LANES = 128
SPLIT = LANES // 2
SUBLANES = 8
MESH = pl.DeviceIdType.MESH


def step_kernel(
    along_wa, along_col, chunks, pieces,
    walkers_hbm, inverse_hbm, noise_hbm, chol_hbm, out_ref, log_ref,
    walkers_ref, inverse_ref, noise_ref,
    chol, green_send, green_recv, part_send, part_recv, half_send, half_recv, v_send, v_recv, total, spread, term, running,
    late, series, tied, late_sum, in_sem, chol_sem, gs, gr, ps, pr, hs, hr, vs, vr,
):
    planes = along_wa * along_col
    count, orbitals, electrons = walkers_ref.shape
    blocks, vectors = chol.shape[0], chol.shape[1]
    rows = blocks * BLOCK
    wide = planes * BLOCK
    deep = vectors * BLOCK
    me = lax.axis_index("wa") * along_col + lax.axis_index("col")
    half = planes // 2
    hops = range(1, planes)
    near, far = range(1, half), range(half, planes)

    def peer(d):
        b = me
        for bit in (1 << i for i in range(planes.bit_length() - 1)):
            if d & bit:
                b = b + bit * (1 - 2 * lax.rem(me // bit, 2))
        return b, {"wa": b // along_col, "col": lax.rem(b, along_col)}

    loads = [
        pltpu.make_async_copy(chol_hbm.at[:, pl.ds(b * BLOCK, BLOCK), :], chol.at[b], chol_sem.at[b])
        for b in range(blocks)
    ]
    barrier = pltpu.get_barrier_semaphore()
    for d in reversed(hops):
        pl.semaphore_signal(barrier, inc=1, device_id=peer(d)[1], device_id_type=MESH)
    inputs = [
        pltpu.make_async_copy(hbm.at[k], ref.at[k], in_sem.at[i, k])
        for k in range(count)
        for i, (hbm, ref) in enumerate(((walkers_hbm, walkers_ref), (inverse_hbm, inverse_ref)))
    ]
    inputs.append(pltpu.make_async_copy(noise_hbm, noise_ref, in_sem.at[2, 0]))
    for load in inputs:
        load.start()

    strip = half * rows

    side = me // half

    def green_of(k, base):
        at = pl.ds(pl.multiple_of(base, strip), strip)
        green_send[k, at, :] = jnp.dot(
            walkers_ref[k, at, :], inverse_ref[k], preferred_element_type=jnp.float32
        ).astype(jnp.bfloat16)

    piece_rows = rows // pieces

    def send_green(k, those):
        for j, d in those:
            b, device = peer(d)
            copy = pltpu.make_async_remote_copy(
                src_ref=green_send.at[k, pl.ds(pl.multiple_of(b * rows + j * piece_rows, BLOCK), piece_rows), :],
                dst_ref=green_recv.at[k, me, pl.ds(j * piece_rows, piece_rows), :],
                send_sem=gs.at[k, d, j],
                recv_sem=gr.at[k, d, j],
                device_id=device,
                device_id_type=MESH,
            )
            copy.start()
            green_copies[k][j].append(copy)

    def keep_green(k):
        green_recv[k, me] = green_send[k, pl.ds(pl.multiple_of(me * rows, rows), rows), :]

    green_copies = [[[] for j in range(pieces)] for k in range(count)]
    across = [(j, d) for j in range(pieces) for d in far]
    beside = [(j, d) for j in range(pieces) for d in near]
    held = len(across) // 2 + 1
    for k in range(count):
        for load in inputs[2 * k : 2 * k + 2]:
            load.wait()
        green_of(k, (1 - side) * strip)
        if k == 0:
            pl.semaphore_wait(barrier, planes - 1)
        if k < 2:
            send_green(k, across if k == 0 else across[:held])
        green_of(k, side * strip)
        if k < 2:
            send_green(k, beside)
        keep_green(k)
    for load in loads:
        load.start()
    for load in (inputs[-1], *loads):
        load.wait()

    row_in = lax.broadcasted_iota(jnp.int32, (deep, wide), 0) % BLOCK
    col_in = lax.broadcasted_iota(jnp.int32, (deep, wide), 1) % BLOCK
    pick = (
        lax.broadcasted_iota(jnp.int32, (planes, wide), 1) // BLOCK
        == lax.broadcasted_iota(jnp.int32, (planes, wide), 0)
    ).astype(jnp.float32)

    def noise_of(k):
        level = (noise_ref[k : k + 1, :].astype(jnp.float32) + 0.5) / NOISE_LEVELS
        return ROOT_TWO * lax.erf_inv(2.0 * level - 1.0)

    def partial_of(k):
        each_piece = blocks // pieces

        def block_dot(i):
            left = chol[i, :, :, :electrons].reshape(deep, electrons)
            right = green_recv[k, :, i * BLOCK : (i + 1) * BLOCK, :].reshape(wide, electrons)
            return lax.dot_general(left, right, (((1,), (1,)), ((), ())), preferred_element_type=jnp.float32)

        for j in range(pieces):
            for copy in green_copies[k][j]:
                copy.wait_recv()
            summed = block_dot(j * each_piece)
            for i in range(j * each_piece + 1, (j + 1) * each_piece):
                summed = summed + block_dot(i)
            total[...] = summed if j == 0 else total[...] + summed
        kept = jnp.where(row_in == col_in, total[...], 0.0).reshape(vectors, BLOCK, wide).sum(axis=1)
        sums = lax.dot_general(
            pick, kept, (((1,), (1,)), ((), ())),
            preferred_element_type=jnp.float32, precision=lax.Precision.HIGHEST,
        )
        own = lax.broadcasted_iota(jnp.int32, (planes, vectors), 0) == me
        part_send[k, :, :vectors] = sums
        part_send[k, :, SPLIT : SPLIT + vectors] = jnp.where(own, noise_of(k), 0.0)

    def send_part(k):
        copies = []
        for d in near:
            copy = pltpu.make_async_remote_copy(
                src_ref=part_send.at[k],
                dst_ref=part_recv.at[k, me],
                send_sem=ps.at[k, d],
                recv_sem=pr.at[k, d],
                device_id=peer(d)[1],
                device_id_type=MESH,
            )
            copy.start()
            copies.append(copy)
        part_recv[k, me] = part_send[k]
        return copies

    half_copies = [
        pltpu.make_async_remote_copy(
            src_ref=half_send.at[k],
            dst_ref=half_recv.at[k],
            send_sem=hs.at[k],
            recv_sem=hr.at[k],
            device_id=peer(half)[1],
            device_id_type=MESH,
        )
        for k in range(count)
    ]

    def send_half(k):
        for copy in part_copies[k]:
            copy.wait_recv()
        summed = part_recv[k, side * half]
        for a in range(1, half):
            summed = summed + part_recv[k, side * half + a]
        half_send[k] = summed
        half_copies[k].start()

    plane_row = lax.broadcasted_iota(jnp.int32, (planes, LANES), 0)
    vector_lane = lax.broadcasted_iota(jnp.int32, (planes, LANES), 1) < SPLIT

    def spread_field(k):
        both = half_send[k] + half_recv[k]
        bias_sum = jnp.where(vector_lane, both, 0.0)
        noise = jnp.where(vector_lane, pltpu.roll(both, LANES - SPLIT, 1), 0.0)
        force = jnp.clip(STEP_ROOT * bias_sum, -BIAS_CAP, BIAS_CAP)
        shifted = noise - force
        steps = jnp.where(plane_row == me, shifted * force - 0.5 * force * force, 0.0)
        log_ref[k] = jnp.sum(steps)
        field = shifted.astype(jnp.bfloat16)
        tall = (
            lax.broadcasted_iota(jnp.int32, (wide, planes), 0) // BLOCK
            == lax.broadcasted_iota(jnp.int32, (wide, planes), 1)
        ).astype(jnp.float32)
        by_row = jnp.dot(tall, field.astype(jnp.float32), preferred_element_type=jnp.float32)
        out = (
            lax.broadcasted_iota(jnp.int32, (LANES, deep), 1) // BLOCK
            == lax.broadcasted_iota(jnp.int32, (LANES, deep), 0)
        ).astype(jnp.float32).astype(jnp.bfloat16)
        both = jnp.dot(by_row.astype(jnp.bfloat16), out, preferred_element_type=jnp.float32)
        same = (
            lax.broadcasted_iota(jnp.int32, (wide, deep), 0) % BLOCK
            == lax.broadcasted_iota(jnp.int32, (wide, deep), 1) % BLOCK
        )
        spread[...] = jnp.where(same, both, 0.0).astype(jnp.bfloat16)

    each = blocks // chunks
    part_rows = each * BLOCK

    def potential_rows(k, c):
        def body(i, carry):
            b = c * each + i
            tile = jnp.dot(
                spread[...], chol[b].reshape(deep, orbitals), preferred_element_type=jnp.float32
            ).astype(jnp.bfloat16)
            v_send[k, :, pl.ds(pl.multiple_of(b * BLOCK, BLOCK), BLOCK), :] = tile.reshape(
                planes, BLOCK, orbitals
            )
            return carry

        lax.fori_loop(0, each, body, 0)

    def mine(c):
        return pl.ds(pl.multiple_of(me * rows + c * part_rows, BLOCK), part_rows)

    final = count - 1
    apart = planes - 1
    late_at = pl.ds(pl.multiple_of(peer(apart)[0] * rows, rows), rows)
    v_recv[final, late_at, :] = jnp.zeros((rows, orbitals), jnp.bfloat16)
    late_copy = pltpu.make_async_remote_copy(
        src_ref=v_send.at[final, peer(apart)[0]],
        dst_ref=late,
        send_sem=vs.at[final, 0, apart],
        recv_sem=vr.at[final, 0, apart],
        device_id=peer(apart)[1],
        device_id_type=MESH,
    )
    near_copies = [[] for k in range(count)]
    far_copies = [[] for k in range(count)]

    def send_rows(k, c, those, kept):
        for d in those:
            b, device = peer(d)
            copy = pltpu.make_async_remote_copy(
                src_ref=v_send.at[k, b, pl.ds(c * part_rows, part_rows), :],
                dst_ref=v_recv.at[k, mine(c), :],
                send_sem=vs.at[k, c, d],
                recv_sem=vr.at[k, c, d],
                device_id=device,
                device_id_type=MESH,
            )
            copy.start()
            kept[k].append(copy)

    def keep_rows(k, c):
        v_recv[k, mine(c), :] = v_send[k, me, pl.ds(c * part_rows, part_rows), :]

    part_send[...] = jnp.zeros_like(part_send)
    part_copies = []

    def bias_of(k):
        partial_of(k)
        part_copies.append(send_part(k))
        send_half(k)

    def field_of(k):
        half_copies[k].wait_recv()
        spread_field(k)

    bias_of(0)
    if count > 1:
        send_green(1, across[held:])
    for k in range(2, count):
        send_green(k, across + beside)
    for k in range(count):
        field_of(k)
        last = k == count - 1
        for c in range(chunks):
            potential_rows(k, c)
            for d, e in zip(range(half, apart), near):
                send_rows(k, c, (d,), far_copies)
                send_rows(k, c, (e,), near_copies)
            if not last:
                send_rows(k, c, (apart,), far_copies)
            keep_rows(k, c)
            if c == 0 and not last:
                bias_of(k + 1)
        if last:
            late_copy.start()

    for k in range(final):
        for degree in range(1, 5):
            def product_rows(base):
                at = pl.ds(pl.multiple_of(base, strip), strip)
                before = walkers_ref[k] if degree == 1 else term[degree % 2]
                product = (-STEP_ROOT / degree) * jnp.dot(
                    v_recv[k, at, :], before, preferred_element_type=jnp.float32
                )
                so_far = walkers_ref[k, at, :].astype(jnp.float32) if degree == 1 else running[at, :]
                if degree == 4:
                    out_ref[k, at, :] = (so_far + product).astype(jnp.bfloat16)
                else:
                    running[at, :] = so_far + product
                    term[(degree + 1) % 2, at, :] = product.astype(jnp.bfloat16)

            if degree == 1:
                for copy in near_copies[k]:
                    copy.wait_recv()
                product_rows(side * strip)
                for copy in far_copies[k]:
                    copy.wait_recv()
                product_rows((1 - side) * strip)
            else:
                product_rows(0)
                product_rows(strip)

    for copy in (*near_copies[final], *far_copies[final]):
        copy.wait_recv()
    scale = [-STEP_ROOT / degree for degree in range(1, 5)]
    halves = [slice(0, strip), slice(strip, 2 * strip)]
    for degree in range(1, 5):
        before = walkers_ref[final] if degree == 1 else series[degree - 2]
        for at in halves:
            product = scale[degree - 1] * jnp.dot(v_recv[final, at, :], before, preferred_element_type=jnp.float32)
            so_far = walkers_ref[final, at, :].astype(jnp.float32) if degree == 1 else running[at, :]
            running[at, :] = so_far + product
            if degree < 4:
                series[degree - 1, at, :] = product.astype(jnp.bfloat16)
    tied[:, :rows] = v_recv[final, :, late_at]
    for power in range(1, 3):
        before = tied[:, (power - 1) * rows : power * rows]
        for at in halves:
            tied[at, power * rows : (power + 1) * rows] = jnp.dot(
                v_recv[final, at, :], before, preferred_element_type=jnp.float32
            ).astype(jnp.bfloat16)

    def times(left, right):
        return jnp.dot(left, right, preferred_element_type=jnp.float32)

    late_copy.wait_recv()
    late_rows = late[...]
    own = late[:, late_at]
    first = scale[0] * times(late_rows, walkers_ref[final])
    term_1 = first.astype(jnp.bfloat16)
    second = scale[1] * (times(late_rows, series[0]) + times(own, term_1))
    term_2 = second.astype(jnp.bfloat16)
    back = times(late_rows, tied[:, : 2 * rows]).astype(jnp.bfloat16)
    third = scale[2] * (
        times(late_rows, series[1]) + scale[1] * times(back[:, :rows], term_1) + times(own, term_2)
    )
    term_3 = third.astype(jnp.bfloat16)
    fourth = scale[3] * (
        times(late_rows, series[2])
        + scale[2] * (scale[1] * times(back[:, rows:], term_1) + times(back[:, :rows], term_2))
        + times(own, term_3)
    )
    late_sum[:rows] = (scale[1] * first + scale[2] * second + scale[3] * third).astype(jnp.bfloat16)
    late_sum[rows : 2 * rows] = (scale[2] * (scale[1] * first + scale[3] * second)).astype(jnp.bfloat16)
    late_sum[2 * rows :] = (scale[3] * scale[2] * scale[1] * first).astype(jnp.bfloat16)
    for at in halves:
        out_ref[final, at, :] = (running[at, :] + times(tied[at, :], late_sum[...])).astype(jnp.bfloat16)
    out_ref[final, late_at, :] = (running[late_at, :] + first + second + third + fourth).astype(jnp.bfloat16)

    for group in (*green_copies, part_copies, [half_copies], near_copies, far_copies, [[late_copy]]):
        for copies in group:
            for copy in copies:
                copy.wait_send()


def per_device(walkers, intersection_inverse, noise_index, cholesky):
    count, orbitals, electrons = walkers.shape
    vectors, rows = cholesky.shape[:2]
    along_wa = lax.axis_size("wa")
    along_col = lax.axis_size("col")
    planes = along_wa * along_col
    if rows % LANES or planes != SUBLANES or vectors > SPLIT:
        return exchange_form(walkers, intersection_inverse, noise_index, cholesky)
    blocks = rows // BLOCK
    chunks = 1
    pieces = 2
    deep, wide = vectors * BLOCK, planes * BLOCK
    vmem = pl.BlockSpec(memory_space=pltpu.VMEM)
    sem = pltpu.SemaphoreType.DMA
    walkers_new, log_weight = pl.pallas_call(
        functools.partial(step_kernel, along_wa, along_col, chunks, pieces),
        out_shape=(
            jax.ShapeDtypeStruct(walkers.shape, jnp.bfloat16),
            jax.ShapeDtypeStruct((count,), jnp.float32),
        ),
        in_specs=[pl.BlockSpec(memory_space=pltpu.HBM)] * 4,
        out_specs=(vmem, pl.BlockSpec(memory_space=pltpu.SMEM)),
        scratch_shapes=[
            pltpu.VMEM(walkers.shape, jnp.bfloat16),
            pltpu.VMEM(intersection_inverse.shape, jnp.bfloat16),
            pltpu.VMEM(noise_index.shape, jnp.int32),
            pltpu.VMEM((blocks, vectors, BLOCK, orbitals), jnp.bfloat16),
            pltpu.VMEM((count, orbitals, electrons), jnp.bfloat16),
            pltpu.VMEM((count, planes, rows, electrons), jnp.bfloat16),
            pltpu.VMEM((count, planes, LANES), jnp.float32),
            pltpu.VMEM((count, planes, planes, LANES), jnp.float32),
            pltpu.VMEM((count, planes, LANES), jnp.float32),
            pltpu.VMEM((count, planes, LANES), jnp.float32),
            pltpu.VMEM((count, planes, rows, orbitals), jnp.bfloat16),
            pltpu.VMEM((count, orbitals, orbitals), jnp.bfloat16),
            pltpu.VMEM((deep, wide), jnp.float32),
            pltpu.VMEM((wide, deep), jnp.bfloat16),
            pltpu.VMEM((2, orbitals, electrons), jnp.bfloat16),
            pltpu.VMEM((orbitals, electrons), jnp.float32),
            pltpu.VMEM((rows, orbitals), jnp.bfloat16),
            pltpu.VMEM((3, orbitals, electrons), jnp.bfloat16),
            pltpu.VMEM((orbitals, 3 * rows), jnp.bfloat16),
            pltpu.VMEM((3 * rows, electrons), jnp.bfloat16),
            sem((3, count)), sem((blocks,)),
            sem((count, planes, pieces)), sem((count, planes, pieces)),
            sem((count, planes)), sem((count, planes)), sem((count,)), sem((count,)),
            sem((count, chunks, planes)), sem((count, chunks, planes)),
        ],
        compiler_params=pltpu.CompilerParams(
            collective_id=0, has_side_effects=True, vmem_limit_bytes=52736 * 1024
        ),
    )(walkers, intersection_inverse, noise_index, cholesky)
    return walkers_new, log_weight


def solution(mesh):
    placed = (
        P(("grp", "wa", "col", "row"), None, None),
        P(("grp", "wa", "col", "row"), None, None),
        P(("grp", "wa", "col", "row"), None),
        P(None, ("wa", "col"), None),
    )
    return jax.shard_map(
        per_device,
        mesh=mesh,
        in_specs=placed,
        out_specs=(P(("grp", "wa", "col", "row"), None, None), P(("grp", "wa", "col", "row"))),
        check_vma=False,
    )
```
